256 devices in a mesh: lon: 32 (over z, y), lat: 8 (over x, core).
Axes of the slice: x: 4, y: 4, z: 8, core: 2. Of those that a mesh axis runs over, the one named last changes fastest.
Arguments:
- fields: float32 [6, 128, 8, 32768], P(None, None, 'lat', 'lon'), may hold values from -6 to 6
- sunlit: int32 [8, 32768], P('lat', 'lon'), may hold values from 0 to 1, as said below
- w_in: bfloat16 [64, 768], replicated, may hold values from -0.21875 to 0.21875
- b_in: float32 [64], replicated, may hold values from -3 to 3
- w_out: bfloat16 [224, 64], replicated, may hold values from -0.75 to 0.75
- b_out: float32 [224], replicated, may hold values from -4 to 4
- level_map: float32 [128, 224], replicated, may hold values from -24 to 24
- dep_owner: int32 [8, 8192, 1], P('lat', 'lon'), may hold values from 0 to 255; in each aligned block of 256 rows (0 to 255, 256 to 511, ..., all dimensions but the last counted through in order) at most 2 rows name the same one
- owner_unit: int32 [8, 8192], P('lat', 'lon'), may hold values from 0 to 255
- h_frac: float32 [8, 8192, 128], P('lat', 'lon'), may hold values from 0 to 1
- h_shift: int32 [8, 8192, 128], P('lat', 'lon'), may hold values from -3 to 3
- v_frac: float32 [8, 256, 128], P('lat', 'lon'), may hold values from 0 to 1
- v_shift: int32 [8, 256, 128], P('lat', 'lon'), may hold values from -2 to 2
Outputs:
- advected: float32 [6, 128, 8, 32768], P(None, None, 'lat', 'lon')
- heating: float32 [128, 8, 32768], P(None, 'lat', 'lon')
The draws below stay inside these ranges and needn't reach their ends.
Inputs may be any that keep to these rules, and one draw needn't show every extreme that they name: At each latitude the sunlit columns form one run, contiguous modulo 32768, of 8192 to 24576 columns, starting at the same column at every latitude. `dep_owner`: the 256 units of one device name no owner more than 2 times, and some device names some owner exactly 2 times.
All inputs are finite; a program needn't handle non-finite values.
Results may differ from the reference program's by a relative error of at most 0.0015.
Values may be sent and summed in bfloat16 or wider, within the bound.
No kernel may reach another device: no remote copies, remote signals or barrier semaphores. Data moves between devices by JAX's collectives and lax.ppermute only.
A program may use at most 128 MiB of HBM per device.

```python
import math
import jax
import jax.numpy as jnp
import numpy as np
from jax import lax

F = 6
LEV = 128
HID = 64
OUT = 224
BLOCK = 128
LG = 4
COLS_DEV = 1024
BLK_DEV = 8
NGRP = 32
UNITS_DEV = 256
CAP = 2
COLUMNS = 32768
N_LON = 32
N_LAT = 8
DEVICES = 256


def draw_sunlit(key, part):
    key_phase, key_width = jax.random.split(key)
    phase = jax.random.randint(key_phase, (), 0, COLUMNS)
    widths = jax.random.randint(key_width, (N_LAT, 1), COLUMNS // 4, 3 * COLUMNS // 4 + 1)
    column_ids = jnp.arange(COLUMNS, dtype=jnp.int32)[None, :]
    return ((column_ids - phase) % COLUMNS < widths).astype(jnp.int32)


def set_ends(array, key, low, high):
    longest = array.shape.index(max(array.shape))
    spots = []
    for shift in (0, 1):
        where = [jax.random.randint(jax.random.fold_in(key, axis), (), 0, length) for axis, length in enumerate(array.shape)]
        where[longest] = (where[longest] + shift) % array.shape[longest]
        spots.append(tuple(where))
    return array.at[spots[0]].set(low).at[spots[1]].set(high)


def levels(rng, shape, cuts, smallest, high):
    factor_of = 1.0
    for dim, blocks in cuts:
        draws = jax.random.uniform(jax.random.fold_in(jax.random.fold_in(rng, 6), dim), (blocks,), jnp.float32, smallest / len(cuts), high / len(cuts))
        factor_of = factor_of * jnp.repeat(jnp.exp(draws), shape[dim] // blocks).reshape((-1,) + (1,) * (len(shape) - 1 - dim))
    return factor_of


def routed_block(rng, own, number, rows, number_of, top, most, slope):
    sequence = jax.random.permutation(rng, number_of)
    heavy_load, usual = shares(number_of, rows * top, most, slope, True), shares(number_of, rows * top, most, slope, False)
    places = jnp.arange(number_of)

    def named(lengths, turn):
        used = int((lengths > 0).sum())
        fixed = max(1, used // 4)
        shifted = fixed + (places - fixed + turn * (used - fixed)) % max(1, number_of - fixed)
        return jnp.zeros((number_of,), jnp.int32).at[sequence[jnp.where(places < fixed, places, shifted)]].set(jnp.asarray(lengths, jnp.int32))

    lengths = jnp.where(number % 4 == 0, named(heavy_load, number // 4), named(usual, number - number // 4 - 1))
    mixed = jax.random.permutation(jax.random.fold_in(own, 3), number_of)
    giver, sink = mixed[0:number_of // 2 * 2:2], mixed[1:number_of // 2 * 2:2]
    margin = jnp.minimum(lengths[giver] - 1, most - lengths[sink]) // 2
    margin = jnp.where((giver == sequence[0]) | (sink == sequence[0]) | (lengths[sink] == 0), 0, jnp.maximum(margin, 0))
    shifted = jax.random.randint(jax.random.fold_in(own, 4), (number_of // 2,), 0, 1 << 20) % (margin + 1)
    lengths = lengths.at[giver].add(-shifted).at[sink].add(shifted)
    labels = jnp.searchsorted(jnp.cumsum(lengths), jnp.arange(rows * top), side="right").astype(jnp.int32)
    grid = labels.reshape(top, rows).T
    grid = grid[jax.random.permutation(jax.random.fold_in(own, 1), rows)]
    turn = jax.random.randint(jax.random.fold_in(own, 2), (rows, 1), 0, top)
    return jnp.take_along_axis(grid, (jnp.arange(top)[None, :] + turn) % top, axis=1)


def shares(number_of, total, bound, slope, full):
    loads = [(1 << 20) // math.isqrt(grade ** slope) + 1 for grade in range(1, number_of + 1)]
    largest = bound if full else min(bound, max(-(-total // number_of), total * loads[0] // sum(loads)))
    least = 1 if total - largest >= number_of - 1 else 0
    counts, spare = [largest] + [least] * (number_of - 1), total - largest - least * (number_of - 1)
    while spare > 0:
        candidates = [i for i in range(1, number_of) if counts[i] < largest] or [i for i in range(1, number_of) if counts[i] < bound]
        whole, left = sum([loads[i] for i in candidates]), spare
        for i in candidates:
            more = min(bound - counts[i], max(1, left * loads[i] // whole), spare)
            counts[i] = counts[i] + more
            spare = spare - more
    return np.array(counts)


def noise(stream_key, dims, width, most, shards=(), kind=jnp.bfloat16):
    level = levels(stream_key, dims, shards, -0.22, 0.18) if shards else 1.0
    values = jax.random.normal(stream_key, dims, jnp.float32) * width * level
    return jnp.minimum(jnp.maximum(values, -most), most).astype(kind)


def setup_inputs(seed: int = 0) -> dict:
    key_list = jax.random.split(jax.random.key(seed), 14)
    fields = noise(key_list[0], (F, LEV, N_LAT, COLUMNS), 1.0, 6.0, ((2, 8), (3, 32)), jnp.float32)
    sunlit = draw_sunlit(jax.random.fold_in(key_list[13], 71), 0)
    w_in = noise(key_list[2], (HID, F * LEV), (F * LEV) ** -0.5, 0.21875)
    b_in = noise(key_list[3], (HID,), 0.5, 3.0, (), jnp.float32)
    w_out = noise(key_list[4], (OUT, HID), HID ** -0.5, 0.75)
    b_out = noise(key_list[5], (OUT,), 0.7, 4.0, (), jnp.float32)
    level_map = noise(key_list[6], (LEV, OUT), 4.0, 24.0, (), jnp.float32)
    dep_owner_keys = jax.random.split(jax.random.fold_in(key_list[7], 1), N_LAT * (N_LON * UNITS_DEV) // UNITS_DEV)
    dep_owner_turns = jax.random.permutation(jax.random.fold_in(key_list[7], 3), N_LAT * (N_LON * UNITS_DEV) // UNITS_DEV)
    dep_owner = jax.vmap(lambda own, number: routed_block(jax.random.fold_in(key_list[7], 2), own, number, UNITS_DEV, DEVICES, 1, CAP, 2))(dep_owner_keys, dep_owner_turns).reshape((N_LAT, N_LON * UNITS_DEV, 1))
    owner_unit = set_ends(jax.random.randint(key_list[8], (N_LAT, N_LON * UNITS_DEV), 0, UNITS_DEV), jax.random.fold_in(key_list[8], 1), 0, UNITS_DEV - 1).astype(jnp.int32)
    h_frac = jnp.clip(1.0 * jax.random.uniform(key_list[9], (N_LAT, N_LON * UNITS_DEV, BLOCK), jnp.float32) ** levels(key_list[9], (N_LAT, N_LON * UNITS_DEV, BLOCK), ((0, 8), (1, 32)), -0.2, 0.2), 0.0, 1.0)
    h_shift = set_ends(jax.random.randint(key_list[10], (N_LAT, N_LON * UNITS_DEV, BLOCK), -3, 4), jax.random.fold_in(key_list[10], 1), -3, 3).astype(jnp.int32)
    v_frac = jnp.clip(1.0 * jax.random.uniform(key_list[11], (N_LAT, N_LON * BLK_DEV, LEV), jnp.float32) ** levels(key_list[11], (N_LAT, N_LON * BLK_DEV, LEV), ((0, 8), (1, 32)), -0.2, 0.2), 0.0, 1.0)
    v_shift = set_ends(jax.random.randint(key_list[12], (N_LAT, N_LON * BLK_DEV, LEV), -2, 3), jax.random.fold_in(key_list[12], 1), -2, 2).astype(jnp.int32)
    return {"fields": fields, "sunlit": sunlit, "w_in": w_in, "b_in": b_in, "w_out": w_out, "b_out": b_out, "level_map": level_map, "dep_owner": dep_owner, "owner_unit": owner_unit, "h_frac": h_frac, "h_shift": h_shift, "v_frac": v_frac, "v_shift": v_shift}


def cubic_weights(fraction):
    return (-fraction * (fraction - 1.0) * (fraction - 2.0) / 6.0,
            (fraction + 1.0) * (fraction - 1.0) * (fraction - 2.0) / 2.0,
            -(fraction + 1.0) * fraction * (fraction - 2.0) / 2.0,
            (fraction + 1.0) * fraction * (fraction - 1.0) / 6.0)


def interp_matrix(fraction, displace, length):
    col_count = fraction.shape[-1]
    position = jnp.arange(col_count, dtype=jnp.int32)
    source = jnp.arange(length, dtype=jnp.int32)[:, None]
    weights = cubic_weights(fraction)
    summed = jnp.zeros(fraction.shape[:-1] + (length, col_count), jnp.float32)
    for offset in range(4):
        stencil = jnp.clip(position + displace + (offset - 1), 0, length - 1).astype(jnp.int32)
        summed = summed + weights[offset][..., None, :] * (source == stencil[..., None, :]).astype(jnp.float32)
    return summed


def column_heating(features, lit_mask, w_in, b_in, w_out, b_out, level_map):
    out_count = w_out.shape[0]
    rows_idx = jnp.arange(out_count, dtype=jnp.int32)
    lower_ones = (rows_idx[:, None] >= rows_idx[None, :]).astype(jnp.float32)
    hidden = jnp.tanh(jnp.dot(w_in, features, preferred_element_type=jnp.float32) + b_in[:, None]).astype(jnp.bfloat16)
    optical = jax.nn.softplus(jnp.dot(w_out, hidden, preferred_element_type=jnp.float32) + b_out[:, None]) * (4.0 / out_count)
    column_depth = jnp.dot(lower_ones, optical, precision=lax.Precision.HIGHEST)
    absorbed = optical * jnp.exp(-column_depth)
    return jnp.dot(level_map, absorbed, precision=lax.Precision.HIGHEST) * lit_mask[None, :]


def reference(fields, sunlit, w_in, b_in, w_out, b_out, level_map, dep_owner, owner_unit, h_frac, h_shift, v_frac, v_shift):
    devices_n = N_LAT * N_LON
    field_grid = fields.reshape(F, LEV, devices_n, COLS_DEV)
    lit_all = sunlit.reshape(devices_n, COLS_DEV).astype(jnp.float32)

    def heat_device(number):
        one_grid = lax.dynamic_index_in_dim(field_grid, number, 2, keepdims=False)
        features = one_grid.reshape(F * LEV, COLS_DEV).astype(jnp.bfloat16)
        lit_mask = lax.dynamic_index_in_dim(lit_all, number, 0, keepdims=False)
        return column_heating(features, lit_mask, w_in, b_in, w_out, b_out, level_map)

    heating = lax.map(heat_device, jnp.arange(devices_n, dtype=jnp.int32))
    warmed = field_grid.at[0].add(heating.transpose(1, 0, 2))
    units_all = warmed.reshape(F, NGRP, LG, devices_n, BLK_DEV, BLOCK).transpose(3, 1, 4, 0, 2, 5)
    units_all = units_all.reshape(devices_n * UNITS_DEV, F, LG, BLOCK)
    sources = (dep_owner.reshape(-1) * UNITS_DEV + owner_unit.reshape(-1)).astype(jnp.int32)
    frac_cols = h_frac.reshape(devices_n, UNITS_DEV, BLOCK)
    shift_cols = h_shift.reshape(devices_n, UNITS_DEV, BLOCK)
    frac_levels = v_frac.reshape(devices_n, BLK_DEV, LEV)
    shift_levels = v_shift.reshape(devices_n, BLK_DEV, LEV)

    def advect_device(number):
        wanted = lax.dynamic_slice_in_dim(sources, number * UNITS_DEV, UNITS_DEV)
        picked = units_all[wanted]
        matrix = interp_matrix(frac_cols[number], shift_cols[number], BLOCK)
        traced = jnp.einsum("ufgr,urc->ufgc", picked, matrix, precision=lax.Precision.HIGHEST)
        regrid = traced.reshape(NGRP, BLK_DEV, F, LG, BLOCK).transpose(2, 0, 3, 1, 4).reshape(F, LEV, BLK_DEV, BLOCK)
        vertical = interp_matrix(frac_levels[number], shift_levels[number], LEV)
        moved = jnp.einsum("blk,flbc->fkbc", vertical, regrid, precision=lax.Precision.HIGHEST)
        return moved.reshape(F, LEV, COLS_DEV)

    advected = lax.map(advect_device, jnp.arange(devices_n, dtype=jnp.int32))
    advected = advected.transpose(1, 2, 0, 3).reshape(F, LEV, N_LAT, N_LON * COLS_DEV)
    heating_out = heating.transpose(1, 0, 2).reshape(LEV, N_LAT, N_LON * COLS_DEV)
    return (advected, heating_out)
```

```python
import functools

import jax
import jax.numpy as jnp
from jax import lax
from jax.experimental import pallas as pl
from jax.experimental.pallas import tpu as pltpu
from jax.sharding import PartitionSpec as P

BLOCK = 128
LG = 4
PAIRS = 3
UNROLL = 16
VERTICAL_UNROLL = 8
PACK_STEPS = 2
AXES = ("lat", "lon")
CODE = 16480.0
SPLIT = 2.0**-75
DECODE = float((65536.0 * CODE) ** -5 / SPLIT)


def cubic_weights(fraction, scale=1.0):
    return (
        -fraction * (fraction - 1.0) * (fraction - 2.0) * (scale / 6.0),
        (fraction + 1.0) * (fraction - 1.0) * (fraction - 2.0) * (scale / 2.0),
        -(fraction + 1.0) * fraction * (fraction - 2.0) * (scale / 2.0),
        (fraction + 1.0) * fraction * (fraction - 1.0) * (scale / 6.0),
    )


def halves(value):
    high = value.astype(jnp.bfloat16)
    return high, (value - high.astype(jnp.float32)).astype(jnp.bfloat16)


def mxu(a, b, a_dim):
    return lax.dot_general(a, b, (((a_dim,), (0,)), ((), ())), preferred_element_type=jnp.float32)


def softplus(v):
    u = jnp.exp(-jnp.abs(v))
    return jnp.maximum(v, 0.0) + jnp.where(
        u < 0.01, u * (1.0 - u * (0.5 - u * (1.0 / 3.0 - u * 0.25))), jnp.log(1.0 + u)
    )


def coded(x):
    root = jnp.exp2(jnp.log2(jnp.abs(x)) * 0.2) * CODE
    return jnp.where(x < 0.0, -root, root)


def nearest(value):
    return jnp.floor(value + 0.5).astype(jnp.int32)


def word_of(first, second):
    low = nearest(coded(second)) & 0xFFFF
    high = nearest(coded(first) - low.astype(jnp.float32) * (1.0 / 65536.0))
    return (high << 16) | low


def heat_kernel(x, sun, w_in, b_in, w_out, b_out, level_map, heat, code):
    outs, levels = level_map.shape
    hid, feats = w_in.shape
    blocks = sun.shape[0]
    width = 2 * BLOCK
    bias_in = jnp.broadcast_to(b_in[...], (width, hid)).T
    bias_out = jnp.broadcast_to(b_out[...], (width, outs)).T
    lower = (
        lax.broadcasted_iota(jnp.int32, (outs, outs), 0)
        >= lax.broadcasted_iota(jnp.int32, (outs, outs), 1)
    ).astype(jnp.float32).astype(jnp.bfloat16)
    map_high, map_low = halves(level_map[...])

    def two_blocks(step, carry):
        b = step * 2
        features = jnp.concatenate(
            [x[pl.ds(b + i, feats, stride=blocks), :] for i in range(2)], axis=1
        ).astype(jnp.bfloat16)
        hidden = jnp.tanh(mxu(w_in[...], features, 1) + bias_in).astype(jnp.bfloat16)
        optical = softplus(mxu(w_out[...], hidden, 0) + bias_out) * (4.0 / outs)
        high, rest = halves(optical)
        middle = (optical - high.astype(jnp.float32)) - rest.astype(jnp.float32)
        depth = mxu(lower, high, 1) + mxu(lower, rest, 1) + mxu(lower, middle.astype(jnp.bfloat16), 1)
        high, rest = halves(optical * jnp.exp(-depth))
        warm = mxu(map_high, high, 0) + mxu(map_high, rest, 0) + mxu(map_low, high, 0)
        for i in range(2):
            lit = sun[pl.ds(b + i, 1), :].astype(jnp.float32)
            heat[pl.ds(b + i, levels, stride=blocks), :] = warm[:, i * BLOCK : (i + 1) * BLOCK] * lit
        return carry

    lax.fori_loop(0, blocks // 2, two_blocks, 0)
    rows = levels * blocks
    chunk = 64

    def code_rows(step, carry):
        at = pl.multiple_of(step * chunk, chunk)
        here = pl.ds(at, chunk)
        for p in range(PAIRS):
            first = x[pl.ds(at + p * rows, chunk), :]
            if p == 0:
                first = first + heat[here, :]
            second = x[pl.ds(at + (p + PAIRS) * rows, chunk), :]
            code[pl.ds(at + p * rows, chunk), :] = word_of(first, second)
        return carry

    lax.fori_loop(0, rows // chunk, code_rows, 0)


def ask_kernel(owner, unit, asked):
    devices = asked.shape[0]
    units = owner.shape[1]
    blocks = 8
    rows = units * LG
    start = (unit[...] // blocks) * (LG * blocks) + unit[...] % blocks
    key = (lax.broadcasted_iota(jnp.int32, (1, units), 1) * rows + start).astype(jnp.float32)
    named = owner[...] == lax.broadcasted_iota(jnp.int32, (devices, units), 0)
    low = jnp.min(jnp.where(named, key, float(units * rows)), axis=1, keepdims=True)
    high = jnp.max(jnp.where(named, key, 0.0), axis=1, keepdims=True)
    low = low.astype(jnp.int32) & (rows - 1)
    high = high.astype(jnp.int32) & (rows - 1)
    asked[...] = jnp.broadcast_to(low | (high << 16), asked.shape)


def pack_kernel(asked, code, sent, row, starts, sem):
    devices = sent.shape[0]
    rows = code.shape[0] // PAIRS

    @pl.when(pl.program_id(0) == 0)
    def _():
        diagonal = lax.broadcasted_iota(jnp.int32, (BLOCK, BLOCK), 0) == lax.broadcasted_iota(
            jnp.int32, (BLOCK, BLOCK), 1
        )
        for i in range(asked.shape[0] // BLOCK):
            tile = jnp.where(diagonal, asked[pl.ds(i * BLOCK, BLOCK), :], 0)
            row[pl.ds(i, 1), :] = jnp.sum(tile, axis=0, keepdims=True)
        copy = pltpu.make_async_copy(row, starts, sem)
        copy.start()
        copy.wait()

    base = pl.program_id(0) * devices

    def one(d, carry):
        owner = base + d
        both = starts[owner >> 7, owner & (BLOCK - 1)]
        for j, at in enumerate((both & 0xFFFF, both >> 16)):
            for p in range(PAIRS):
                sent[d, pl.ds((j * PAIRS + p) * LG, LG), :] = code[
                    pl.ds(at + p * rows, LG, stride=8), :
                ]
        return carry

    lax.fori_loop(0, devices, one, 0, unroll=16)


def prepare_kernel(h_frac, h_shift, v_frac, v_shift, weights, places, v_high, v_low):
    units = h_frac.shape[0]
    blocks, levels = v_frac.shape
    lane = lax.broadcasted_iota(jnp.int32, (units, BLOCK), 1)
    for k, weight in enumerate(cubic_weights(h_frac[...])):
        weights[pl.ds(k * units, units), :] = weight * DECODE
        places[pl.ds(k * units, units), :] = jnp.clip(lane + h_shift[...] + (k - 1), 0, BLOCK - 1)
    source = lax.broadcasted_iota(jnp.int32, (levels, levels), 0)
    target = lax.broadcasted_iota(jnp.int32, (1, levels), 1)

    def one_block(b, carry):
        vertical = jnp.zeros((levels, levels), jnp.float32)
        shift = v_shift[pl.ds(b, 1), :]
        for j, weight in enumerate(cubic_weights(v_frac[pl.ds(b, 1), :])):
            at = jnp.clip(target + shift + (j - 1), 0, levels - 1)
            vertical = vertical + jnp.where(source == at, weight * SPLIT, 0.0)
        high, low = halves(vertical.T)
        here = pl.ds(pl.multiple_of(b * levels, levels), levels)
        v_high[here, :] = high
        v_low[here, :] = low
        return carry

    lax.fori_loop(0, blocks, one_block, 0)


def lanes_at(value, index):
    numbers = lax.GatherDimensionNumbers(
        offset_dims=(),
        collapsed_slice_dims=(1,),
        start_index_map=(1,),
        operand_batching_dims=(0,),
        start_indices_batching_dims=(0,),
    )
    return lax.gather(
        value, index[..., None], numbers, (1, 1), mode=lax.GatherScatterMode.PROMISE_IN_BOUNDS
    )


def fifth_times(word, weight):
    y = word.astype(jnp.float32)
    square = y * y
    return (y * weight) * square * square


def advect_kernel(landing, got, weights, places, v_high, v_low, out, traced, moved_all, sems):
    units = places.shape[0] // 4
    levels = v_high.shape[1]
    blocks = v_high.shape[0] // levels
    groups = levels // LG
    rows = levels * blocks
    fields = 2 * PAIRS
    upper = lax.broadcasted_iota(jnp.int32, (2 * LG, BLOCK), 0) < LG

    def one_block(b, carry):
        base = b * (fields * levels)

        def two_units(step, inner):
            unit = [(step * 2 + i) * blocks + b for i in range(2)]
            row = [landing[u] * (PAIRS * LG) for u in unit]
            tails = [got[pl.ds(r + LG, 2 * LG), :] for r in row]
            words = [got[pl.ds(r, 2 * LG), :] for r in row]
            words.append(jnp.where(upper, pltpu.roll(tails[0], LG, 0), tails[1]))
            sums = [None] * 6
            for k in range(4):
                index = [places[pl.ds(u + k * units, 2 * LG, stride=0), :] for u in unit]
                weight = [weights[pl.ds(u + k * units, 2 * LG, stride=0), :] for u in unit]
                index.append(jnp.where(upper, index[0], index[1]))
                weight.append(jnp.where(upper, weight[0], weight[1]))
                for n in range(3):
                    word = lanes_at(words[n], index[n])
                    for half, part in enumerate((word, word << 16)):
                        term = fifth_times(part, weight[n])
                        at = n * 2 + half
                        sums[at] = term if k == 0 else sums[at] + term
            for n in range(2):
                for half in range(2):
                    for i in range(2):
                        f = i + half * PAIRS
                        traced[pl.ds(base + f * levels + (step * 2 + n) * LG, LG), :] = sums[n * 2 + half][
                            i * LG : (i + 1) * LG
                        ]
            for half in range(2):
                f = 2 + half * PAIRS
                at = pl.multiple_of(base + f * levels + step * 2 * LG, 2 * LG)
                traced[pl.ds(at, 2 * LG), :] = sums[4 + half]
            return inner

        lax.fori_loop(0, groups // 2, two_units, 0, unroll=UNROLL)
        return carry

    lax.fori_loop(0, blocks, one_block, 0)
    copies = []
    for first in range(0, fields, 2):

        def one_vertical(b, carry):
            at = pl.multiple_of(b * (fields * levels), levels)
            wide = jnp.concatenate(
                [traced[pl.ds(at + (first + i) * levels, levels), :] for i in range(2)], axis=1
            )
            t_high, t_low = halves(wide)
            here = pl.ds(pl.multiple_of(b * levels, levels), levels)
            high, low = v_high[here, :], v_low[here, :]
            moved = mxu(
                jnp.concatenate([high, high], axis=1), jnp.concatenate([t_high, t_low], axis=0), 1
            ) + mxu(low, t_high, 1)
            for i in range(2):
                moved_all[pl.ds((first + i) * rows + b, levels, stride=blocks), :] = moved[
                    :, i * BLOCK : (i + 1) * BLOCK
                ]
            return carry

        lax.fori_loop(0, blocks, one_vertical, 0, unroll=VERTICAL_UNROLL)
        here = pl.ds(first * rows, 2 * rows)
        copies.append(pltpu.make_async_copy(moved_all.at[here, :], out.at[here, :], sems.at[first // 2]))
        copies[-1].start()
    for copy in copies:
        copy.wait()


VMEM = pl.BlockSpec(memory_space=pltpu.VMEM)
SMEM = pl.BlockSpec(memory_space=pltpu.SMEM)
ANY = pl.BlockSpec(memory_space=pl.ANY)


def keep_near(value):
    return pltpu.with_memory_space_constraint(value, pltpu.VMEM)


def exchange(value):
    return lax.all_to_all(value, AXES, split_axis=0, concat_axis=0, tiled=True)


def heat(fields, sunlit, w_in, b_in, w_out, b_out, level_map):
    n_fields, levels, _, columns = fields.shape
    blocks = columns // BLOCK
    rows = levels * blocks
    return pl.pallas_call(
        heat_kernel,
        out_shape=(
            jax.ShapeDtypeStruct((rows, BLOCK), jnp.float32),
            jax.ShapeDtypeStruct((PAIRS * rows, BLOCK), jnp.int32),
        ),
        in_specs=[VMEM] * 7,
        out_specs=(VMEM, VMEM),
        compiler_params=pltpu.CompilerParams(vmem_limit_bytes=20 << 20),
        name="heat",
    )(
        fields.reshape(n_fields * rows, BLOCK),
        sunlit.reshape(blocks, BLOCK),
        w_in,
        b_in.reshape(1, -1),
        w_out.T,
        b_out.reshape(1, -1),
        level_map.T,
    )


def ask(owner, unit, devices):
    return pl.pallas_call(
        ask_kernel,
        out_shape=jax.ShapeDtypeStruct((devices, BLOCK), jnp.int32),
        in_specs=[VMEM] * 2,
        out_specs=VMEM,
        compiler_params=pltpu.CompilerParams(vmem_limit_bytes=8 << 20),
        name="ask",
    )(owner, unit)


def pack(asked, code):
    devices = asked.shape[0]
    shape = (devices, 2 * PAIRS * LG, BLOCK)
    return pl.pallas_call(
        pack_kernel,
        grid=(PACK_STEPS,),
        out_shape=jax.ShapeDtypeStruct(shape, jnp.int32),
        in_specs=[VMEM] * 2,
        out_specs=pl.BlockSpec((devices // PACK_STEPS,) + shape[1:], lambda i: (i, 0, 0)),
        scratch_shapes=[
            pltpu.VMEM((devices // BLOCK, BLOCK), jnp.int32),
            pltpu.SMEM((devices // BLOCK, BLOCK), jnp.int32),
            pltpu.SemaphoreType.DMA,
        ],
        compiler_params=pltpu.CompilerParams(vmem_limit_bytes=12 << 20),
        name="pack",
    )(keep_near(asked), keep_near(code))


def prepare(h_frac, h_shift, v_frac, v_shift):
    units = h_frac.shape[0]
    blocks, levels = v_frac.shape
    return pl.pallas_call(
        prepare_kernel,
        out_shape=(
            jax.ShapeDtypeStruct((4 * units, BLOCK), jnp.float32),
            jax.ShapeDtypeStruct((4 * units, BLOCK), jnp.int32),
            jax.ShapeDtypeStruct((blocks * levels, levels), jnp.bfloat16),
            jax.ShapeDtypeStruct((blocks * levels, levels), jnp.bfloat16),
        ),
        in_specs=[VMEM] * 4,
        out_specs=(VMEM,) * 4,
        compiler_params=pltpu.CompilerParams(vmem_limit_bytes=12 << 20),
        name="prepare",
    )(h_frac, h_shift, v_frac, v_shift)


def advect(landing, got, prepared):
    levels = prepared[2].shape[1]
    rows = prepared[2].shape[0]
    fields = 2 * PAIRS
    return pl.pallas_call(
        advect_kernel,
        out_shape=jax.ShapeDtypeStruct((fields * rows, BLOCK), jnp.float32),
        in_specs=[SMEM] + [VMEM] * 5,
        out_specs=ANY,
        scratch_shapes=[
            pltpu.VMEM((fields * rows, BLOCK), jnp.float32),
            pltpu.VMEM((fields * rows, BLOCK), jnp.float32),
            pltpu.SemaphoreType.DMA((PAIRS,)),
        ],
        compiler_params=pltpu.CompilerParams(vmem_limit_bytes=24 << 20),
        name="advect",
    )(landing, keep_near(got.reshape(-1, BLOCK)), *[keep_near(p) for p in prepared])


def per_device(
    fields,
    sunlit,
    w_in,
    b_in,
    w_out,
    b_out,
    level_map,
    dep_owner,
    owner_unit,
    h_frac,
    h_shift,
    v_frac,
    v_shift,
):
    n_fields, levels, _, columns = fields.shape
    units = owner_unit.shape[1]
    devices = lax.axis_size("lat") * lax.axis_size("lon")
    owners = dep_owner[0, :, 0]
    order = jnp.arange(units, dtype=jnp.int32)
    asked = exchange(ask(owners.reshape(1, units), owner_unit, devices)[:, None, :])
    second = jnp.any((owners[:, None] == owners[None, :]) & (order[:, None] > order[None, :]), axis=1)
    landing = owners * 2 + second.astype(jnp.int32)
    heating, code = heat(fields, sunlit, w_in, b_in, w_out, b_out, level_map)
    got = exchange(pack(asked.reshape(devices, BLOCK), code))
    prepared = prepare(h_frac[0], h_shift[0], v_frac[0], v_shift[0])
    advected = advect(landing, got, prepared)
    return (advected.reshape(n_fields, levels, 1, columns), heating.reshape(levels, 1, columns))


def solution(mesh):
    placed = (
        P(None, None, "lat", "lon"),
        P("lat", "lon"),
        P(),
        P(),
        P(),
        P(),
        P(),
        P("lat", "lon", None),
        P("lat", "lon"),
        P("lat", "lon", None),
        P("lat", "lon", None),
        P("lat", "lon", None),
        P("lat", "lon", None),
    )
    return jax.shard_map(
        per_device,
        mesh=mesh,
        in_specs=placed,
        out_specs=(P(None, None, "lat", "lon"), P(None, "lat", "lon")),
        check_vma=False,
    )
```

```python
import functools

import jax
import jax.numpy as jnp
from jax import lax
from jax.experimental import pallas as pl
from jax.experimental.pallas import tpu as pltpu
from jax.sharding import PartitionSpec as P

BLOCK = 128
LG = 4
PAIRS = 3
UNROLL = 16
VERTICAL_UNROLL = 8
PACK_STEPS = 8
AXES = ("lat", "lon")
CODE = 16480.0
SPLIT = 2.0**-75
DECODE = float((65536.0 * CODE) ** -5 / SPLIT)


def cubic_weights(fraction, scale=1.0):
    return (
        -fraction * (fraction - 1.0) * (fraction - 2.0) * (scale / 6.0),
        (fraction + 1.0) * (fraction - 1.0) * (fraction - 2.0) * (scale / 2.0),
        -(fraction + 1.0) * fraction * (fraction - 2.0) * (scale / 2.0),
        (fraction + 1.0) * fraction * (fraction - 1.0) * (scale / 6.0),
    )


def halves(value):
    high = value.astype(jnp.bfloat16)
    return high, (value - high.astype(jnp.float32)).astype(jnp.bfloat16)


def mxu(a, b, a_dim):
    return lax.dot_general(a, b, (((a_dim,), (0,)), ((), ())), preferred_element_type=jnp.float32)


def softplus(v):
    u = jnp.exp(-jnp.abs(v))
    return jnp.maximum(v, 0.0) + jnp.where(
        u < 0.01, u * (1.0 - u * (0.5 - u * (1.0 / 3.0 - u * 0.25))), jnp.log(1.0 + u)
    )


def coded(x):
    root = jnp.exp2(jnp.log2(jnp.abs(x)) * 0.2) * CODE
    return jnp.where(x < 0.0, -root, root)


def nearest(value):
    return jnp.floor(value + 0.5).astype(jnp.int32)


def word_of(first, second):
    low = nearest(coded(second)) & 0xFFFF
    high = nearest(coded(first) - low.astype(jnp.float32) * (1.0 / 65536.0))
    return (high << 16) | low


def heat_kernel(x, sun, w_in, b_in, w_out, b_out, level_map, heat, code):
    outs, levels = level_map.shape
    hid, feats = w_in.shape
    blocks = sun.shape[0]
    width = 2 * BLOCK
    bias_in = jnp.broadcast_to(b_in[...], (width, hid)).T
    bias_out = jnp.broadcast_to(b_out[...], (width, outs)).T
    lower = (
        lax.broadcasted_iota(jnp.int32, (outs, outs), 0)
        >= lax.broadcasted_iota(jnp.int32, (outs, outs), 1)
    ).astype(jnp.float32).astype(jnp.bfloat16)
    map_high, map_low = halves(level_map[...])

    def two_blocks(step, carry):
        b = step * 2
        features = jnp.concatenate(
            [x[pl.ds(b + i, feats, stride=blocks), :] for i in range(2)], axis=1
        ).astype(jnp.bfloat16)
        hidden = jnp.tanh(mxu(w_in[...], features, 1) + bias_in).astype(jnp.bfloat16)
        optical = softplus(mxu(w_out[...], hidden, 0) + bias_out) * (4.0 / outs)
        high, rest = halves(optical)
        middle = (optical - high.astype(jnp.float32)) - rest.astype(jnp.float32)
        depth = mxu(lower, high, 1) + mxu(lower, rest, 1) + mxu(lower, middle.astype(jnp.bfloat16), 1)
        high, rest = halves(optical * jnp.exp(-depth))
        warm = mxu(map_high, high, 0) + mxu(map_high, rest, 0) + mxu(map_low, high, 0)
        for i in range(2):
            lit = sun[pl.ds(b + i, 1), :].astype(jnp.float32)
            heat[pl.ds(b + i, levels, stride=blocks), :] = warm[:, i * BLOCK : (i + 1) * BLOCK] * lit
        return carry

    lax.fori_loop(0, blocks // 2, two_blocks, 0)
    rows = levels * blocks
    chunk = 64

    def code_rows(step, carry):
        at = pl.multiple_of(step * chunk, chunk)
        here = pl.ds(at, chunk)
        for p in range(PAIRS):
            first = x[pl.ds(at + p * rows, chunk), :]
            if p == 0:
                first = first + heat[here, :]
            second = x[pl.ds(at + (p + PAIRS) * rows, chunk), :]
            code[pl.ds(at + p * rows, chunk), :] = word_of(first, second)
        return carry

    lax.fori_loop(0, rows // chunk, code_rows, 0)


def ask_kernel(owner, unit, asked):
    devices = asked.shape[0]
    units = owner.shape[1]
    blocks = 8
    rows = units * LG
    start = (unit[...] // blocks) * (LG * blocks) + unit[...] % blocks
    key = (lax.broadcasted_iota(jnp.int32, (1, units), 1) * rows + start).astype(jnp.float32)
    named = owner[...] == lax.broadcasted_iota(jnp.int32, (devices, units), 0)
    low = jnp.min(jnp.where(named, key, float(units * rows)), axis=1, keepdims=True)
    high = jnp.max(jnp.where(named, key, 0.0), axis=1, keepdims=True)
    low = low.astype(jnp.int32) & (rows - 1)
    high = high.astype(jnp.int32) & (rows - 1)
    asked[...] = jnp.broadcast_to(low | (high << 16), asked.shape)


def pack_kernel(asked, code, sent, row, starts, sem):
    devices = sent.shape[0]
    rows = code.shape[0] // PAIRS

    @pl.when(pl.program_id(0) == 0)
    def _():
        diagonal = lax.broadcasted_iota(jnp.int32, (BLOCK, BLOCK), 0) == lax.broadcasted_iota(
            jnp.int32, (BLOCK, BLOCK), 1
        )
        for i in range(asked.shape[0] // BLOCK):
            tile = jnp.where(diagonal, asked[pl.ds(i * BLOCK, BLOCK), :], 0)
            row[pl.ds(i, 1), :] = jnp.sum(tile, axis=0, keepdims=True)
        copy = pltpu.make_async_copy(row, starts, sem)
        copy.start()
        copy.wait()

    base = pl.program_id(0) * devices

    def one(d, carry):
        owner = base + d
        both = starts[owner >> 7, owner & (BLOCK - 1)]
        for j, at in enumerate((both & 0xFFFF, both >> 16)):
            for p in range(PAIRS):
                sent[d, pl.ds((j * PAIRS + p) * LG, LG), :] = code[
                    pl.ds(at + p * rows, LG, stride=8), :
                ]
        return carry

    lax.fori_loop(0, devices, one, 0, unroll=16)


def prepare_kernel(h_frac, h_shift, v_frac, v_shift, weights, places, v_high, v_low):
    units = h_frac.shape[0]
    blocks, levels = v_frac.shape
    lane = lax.broadcasted_iota(jnp.int32, (units, BLOCK), 1)
    for k, weight in enumerate(cubic_weights(h_frac[...])):
        weights[pl.ds(k * units, units), :] = weight * DECODE
        places[pl.ds(k * units, units), :] = jnp.clip(lane + h_shift[...] + (k - 1), 0, BLOCK - 1)
    source = lax.broadcasted_iota(jnp.int32, (levels, levels), 0)
    target = lax.broadcasted_iota(jnp.int32, (1, levels), 1)

    def one_block(b, carry):
        vertical = jnp.zeros((levels, levels), jnp.float32)
        shift = v_shift[pl.ds(b, 1), :]
        for j, weight in enumerate(cubic_weights(v_frac[pl.ds(b, 1), :])):
            at = jnp.clip(target + shift + (j - 1), 0, levels - 1)
            vertical = vertical + jnp.where(source == at, weight * SPLIT, 0.0)
        high, low = halves(vertical.T)
        here = pl.ds(pl.multiple_of(b * levels, levels), levels)
        v_high[here, :] = high
        v_low[here, :] = low
        return carry

    lax.fori_loop(0, blocks, one_block, 0)


def lanes_at(value, index):
    numbers = lax.GatherDimensionNumbers(
        offset_dims=(),
        collapsed_slice_dims=(1,),
        start_index_map=(1,),
        operand_batching_dims=(0,),
        start_indices_batching_dims=(0,),
    )
    return lax.gather(
        value, index[..., None], numbers, (1, 1), mode=lax.GatherScatterMode.PROMISE_IN_BOUNDS
    )


def fifth_times(word, weight):
    y = word.astype(jnp.float32)
    square = y * y
    return (y * weight) * square * square


def advect_kernel(landing, got, weights, places, v_high, v_low, out, traced, moved_all, sems):
    units = places.shape[0] // 4
    levels = v_high.shape[1]
    blocks = v_high.shape[0] // levels
    groups = levels // LG
    rows = levels * blocks
    fields = 2 * PAIRS
    upper = lax.broadcasted_iota(jnp.int32, (2 * LG, BLOCK), 0) < LG

    def one_block(b, carry):
        base = b * (fields * levels)

        def two_units(step, inner):
            unit = [(step * 2 + i) * blocks + b for i in range(2)]
            row = [landing[u] * (PAIRS * LG) for u in unit]
            tails = [got[pl.ds(r + LG, 2 * LG), :] for r in row]
            words = [got[pl.ds(r, 2 * LG), :] for r in row]
            words.append(jnp.where(upper, pltpu.roll(tails[0], LG, 0), tails[1]))
            sums = [None] * 6
            for k in range(4):
                index = [places[pl.ds(u + k * units, 2 * LG, stride=0), :] for u in unit]
                weight = [weights[pl.ds(u + k * units, 2 * LG, stride=0), :] for u in unit]
                index.append(jnp.where(upper, index[0], index[1]))
                weight.append(jnp.where(upper, weight[0], weight[1]))
                for n in range(3):
                    word = lanes_at(words[n], index[n])
                    for half, part in enumerate((word, word << 16)):
                        term = fifth_times(part, weight[n])
                        at = n * 2 + half
                        sums[at] = term if k == 0 else sums[at] + term
            for n in range(2):
                for half in range(2):
                    for i in range(2):
                        f = i + half * PAIRS
                        traced[pl.ds(base + f * levels + (step * 2 + n) * LG, LG), :] = sums[n * 2 + half][
                            i * LG : (i + 1) * LG
                        ]
            for half in range(2):
                f = 2 + half * PAIRS
                at = pl.multiple_of(base + f * levels + step * 2 * LG, 2 * LG)
                traced[pl.ds(at, 2 * LG), :] = sums[4 + half]
            return inner

        lax.fori_loop(0, groups // 2, two_units, 0, unroll=UNROLL)
        return carry

    lax.fori_loop(0, blocks, one_block, 0)
    copies = []
    for first in range(0, fields, 2):

        def one_vertical(b, carry):
            at = pl.multiple_of(b * (fields * levels), levels)
            wide = jnp.concatenate(
                [traced[pl.ds(at + (first + i) * levels, levels), :] for i in range(2)], axis=1
            )
            t_high, t_low = halves(wide)
            here = pl.ds(pl.multiple_of(b * levels, levels), levels)
            high, low = v_high[here, :], v_low[here, :]
            moved = mxu(
                jnp.concatenate([high, high], axis=1), jnp.concatenate([t_high, t_low], axis=0), 1
            ) + mxu(low, t_high, 1)
            for i in range(2):
                moved_all[pl.ds((first + i) * rows + b, levels, stride=blocks), :] = moved[
                    :, i * BLOCK : (i + 1) * BLOCK
                ]
            return carry

        lax.fori_loop(0, blocks, one_vertical, 0, unroll=VERTICAL_UNROLL)
        here = pl.ds(first * rows, 2 * rows)
        copies.append(pltpu.make_async_copy(moved_all.at[here, :], out.at[here, :], sems.at[first // 2]))
        copies[-1].start()
    for copy in copies:
        copy.wait()


VMEM = pl.BlockSpec(memory_space=pltpu.VMEM)
SMEM = pl.BlockSpec(memory_space=pltpu.SMEM)
ANY = pl.BlockSpec(memory_space=pl.ANY)


def keep_near(value):
    return pltpu.with_memory_space_constraint(value, pltpu.VMEM)


def exchange(value):
    return lax.all_to_all(value, AXES, split_axis=0, concat_axis=0, tiled=True)


def heat(fields, sunlit, w_in, b_in, w_out, b_out, level_map):
    n_fields, levels, _, columns = fields.shape
    blocks = columns // BLOCK
    rows = levels * blocks
    return pl.pallas_call(
        heat_kernel,
        out_shape=(
            jax.ShapeDtypeStruct((rows, BLOCK), jnp.float32),
            jax.ShapeDtypeStruct((PAIRS * rows, BLOCK), jnp.int32),
        ),
        in_specs=[VMEM] * 7,
        out_specs=(VMEM, VMEM),
        compiler_params=pltpu.CompilerParams(vmem_limit_bytes=20 << 20),
        name="heat",
    )(
        *map(
            keep_far,
            (
                fields.reshape(n_fields * rows, BLOCK),
                sunlit.reshape(blocks, BLOCK),
                w_in,
                b_in.reshape(1, -1),
                w_out.T,
                b_out.reshape(1, -1),
                level_map.T,
            ),
        )
    )


def keep_far(value):
    return pltpu.with_memory_space_constraint(value, pltpu.HBM)


def ask(owner, unit, devices):
    return pl.pallas_call(
        ask_kernel,
        out_shape=jax.ShapeDtypeStruct((devices, BLOCK), jnp.int32),
        in_specs=[VMEM] * 2,
        out_specs=VMEM,
        name="ask",
    )(owner, unit)


def pack(asked, code):
    devices = asked.shape[0]
    shape = (devices, 2 * PAIRS * LG, BLOCK)
    return pl.pallas_call(
        pack_kernel,
        grid=(PACK_STEPS,),
        out_shape=jax.ShapeDtypeStruct(shape, jnp.int32),
        in_specs=[VMEM] * 2,
        out_specs=pl.BlockSpec((devices // PACK_STEPS,) + shape[1:], lambda i: (i, 0, 0)),
        scratch_shapes=[
            pltpu.VMEM((devices // BLOCK, BLOCK), jnp.int32),
            pltpu.SMEM((devices // BLOCK, BLOCK), jnp.int32),
            pltpu.SemaphoreType.DMA,
        ],
        compiler_params=pltpu.CompilerParams(vmem_limit_bytes=12 << 20),
        name="pack",
    )(keep_near(asked), keep_near(code))


def prepare(h_frac, h_shift, v_frac, v_shift):
    units = h_frac.shape[0]
    blocks, levels = v_frac.shape
    return pl.pallas_call(
        prepare_kernel,
        out_shape=(
            jax.ShapeDtypeStruct((4 * units, BLOCK), jnp.float32),
            jax.ShapeDtypeStruct((4 * units, BLOCK), jnp.int32),
            jax.ShapeDtypeStruct((blocks * levels, levels), jnp.bfloat16),
            jax.ShapeDtypeStruct((blocks * levels, levels), jnp.bfloat16),
        ),
        in_specs=[VMEM] * 4,
        out_specs=(VMEM,) * 4,
        name="prepare",
    )(h_frac, h_shift, v_frac, v_shift)


def advect(landing, got, prepared):
    levels = prepared[2].shape[1]
    rows = prepared[2].shape[0]
    fields = 2 * PAIRS
    return pl.pallas_call(
        advect_kernel,
        out_shape=jax.ShapeDtypeStruct((fields * rows, BLOCK), jnp.float32),
        in_specs=[SMEM] + [VMEM] * 5,
        out_specs=ANY,
        scratch_shapes=[
            pltpu.VMEM((fields * rows, BLOCK), jnp.float32),
            pltpu.VMEM((fields * rows, BLOCK), jnp.float32),
            pltpu.SemaphoreType.DMA((PAIRS,)),
        ],
        name="advect",
    )(landing, keep_near(got.reshape(-1, BLOCK)), *prepared)


def per_device(
    fields,
    sunlit,
    w_in,
    b_in,
    w_out,
    b_out,
    level_map,
    dep_owner,
    owner_unit,
    h_frac,
    h_shift,
    v_frac,
    v_shift,
):
    n_fields, levels, _, columns = fields.shape
    units = owner_unit.shape[1]
    devices = lax.axis_size("lat") * lax.axis_size("lon")
    owners = dep_owner[0, :, 0]
    order = jnp.arange(units, dtype=jnp.int32)
    asked = exchange(ask(owners.reshape(1, units), owner_unit, devices)[:, None, :])
    second = jnp.any((owners[:, None] == owners[None, :]) & (order[:, None] > order[None, :]), axis=1)
    landing = owners * 2 + second.astype(jnp.int32)
    heating, code = heat(fields, sunlit, w_in, b_in, w_out, b_out, level_map)
    got = exchange(pack(asked.reshape(devices, BLOCK), code))
    prepared = prepare(h_frac[0], h_shift[0], v_frac[0], v_shift[0])
    advected = advect(landing, got, prepared)
    return (advected.reshape(n_fields, levels, 1, columns), heating.reshape(levels, 1, columns))


def solution(mesh):
    placed = (
        P(None, None, "lat", "lon"),
        P("lat", "lon"),
        P(),
        P(),
        P(),
        P(),
        P(),
        P("lat", "lon", None),
        P("lat", "lon"),
        P("lat", "lon", None),
        P("lat", "lon", None),
        P("lat", "lon", None),
        P("lat", "lon", None),
    )
    return jax.shard_map(
        per_device,
        mesh=mesh,
        in_specs=placed,
        out_specs=(P(None, None, "lat", "lon"), P(None, "lat", "lon")),
        check_vma=False,
    )
```

```python
import functools

import jax
import jax.numpy as jnp
from jax import lax
from jax.experimental import pallas as pl
from jax.experimental.pallas import tpu as pltpu
from jax.sharding import PartitionSpec as P

BLOCK = 128
LG = 4
PAIRS = 3
UNROLL = 16
VERTICAL_UNROLL = 8
PACK_STEPS = 4
AXES = ("lat", "lon")
CODE = 16480.0
SPLIT = 2.0**-75
DECODE = float((65536.0 * CODE) ** -5 / SPLIT)


def cubic_weights(fraction, scale=1.0):
    return (
        -fraction * (fraction - 1.0) * (fraction - 2.0) * (scale / 6.0),
        (fraction + 1.0) * (fraction - 1.0) * (fraction - 2.0) * (scale / 2.0),
        -(fraction + 1.0) * fraction * (fraction - 2.0) * (scale / 2.0),
        (fraction + 1.0) * fraction * (fraction - 1.0) * (scale / 6.0),
    )


def halves(value):
    high = value.astype(jnp.bfloat16)
    return high, (value - high.astype(jnp.float32)).astype(jnp.bfloat16)


def mxu(a, b, a_dim):
    return lax.dot_general(a, b, (((a_dim,), (0,)), ((), ())), preferred_element_type=jnp.float32)


def softplus(v):
    u = jnp.exp(-jnp.abs(v))
    return jnp.maximum(v, 0.0) + jnp.where(
        u < 0.01, u * (1.0 - u * (0.5 - u * (1.0 / 3.0 - u * 0.25))), jnp.log(1.0 + u)
    )


def coded(x):
    root = jnp.exp2(jnp.log2(jnp.abs(x)) * 0.2) * CODE
    return jnp.where(x < 0.0, -root, root)


def nearest(value):
    return jnp.floor(value + 0.5).astype(jnp.int32)


def word_of(first, second):
    low = nearest(coded(second)) & 0xFFFF
    high = nearest(coded(first) - low.astype(jnp.float32) * (1.0 / 65536.0))
    return (high << 16) | low


def heat_kernel(x, sun, w_in, b_in, w_out, b_out, level_map, heat, code):
    outs, levels = level_map.shape
    hid, feats = w_in.shape
    blocks = sun.shape[0]
    width = 2 * BLOCK
    bias_in = jnp.broadcast_to(b_in[...], (width, hid)).T
    bias_out = jnp.broadcast_to(b_out[...], (width, outs)).T
    lower = (
        lax.broadcasted_iota(jnp.int32, (outs, outs), 0)
        >= lax.broadcasted_iota(jnp.int32, (outs, outs), 1)
    ).astype(jnp.float32).astype(jnp.bfloat16)
    map_high, map_low = halves(level_map[...])

    def two_blocks(step, carry):
        b = step * 2
        features = jnp.concatenate(
            [x[pl.ds(b + i, feats, stride=blocks), :] for i in range(2)], axis=1
        ).astype(jnp.bfloat16)
        hidden = jnp.tanh(mxu(w_in[...], features, 1) + bias_in).astype(jnp.bfloat16)
        optical = softplus(mxu(w_out[...], hidden, 0) + bias_out) * (4.0 / outs)
        high, rest = halves(optical)
        middle = (optical - high.astype(jnp.float32)) - rest.astype(jnp.float32)
        depth = mxu(lower, high, 1) + mxu(lower, rest, 1) + mxu(lower, middle.astype(jnp.bfloat16), 1)
        high, rest = halves(optical * jnp.exp(-depth))
        warm = mxu(map_high, high, 0) + mxu(map_high, rest, 0) + mxu(map_low, high, 0)
        for i in range(2):
            lit = sun[pl.ds(b + i, 1), :].astype(jnp.float32)
            heat[pl.ds(b + i, levels, stride=blocks), :] = warm[:, i * BLOCK : (i + 1) * BLOCK] * lit
        return carry

    lax.fori_loop(0, blocks // 2, two_blocks, 0)
    rows = levels * blocks
    chunk = 64

    def code_rows(step, carry):
        at = pl.multiple_of(step * chunk, chunk)
        here = pl.ds(at, chunk)
        for p in range(PAIRS):
            first = x[pl.ds(at + p * rows, chunk), :]
            if p == 0:
                first = first + heat[here, :]
            second = x[pl.ds(at + (p + PAIRS) * rows, chunk), :]
            code[pl.ds(at + p * rows, chunk), :] = word_of(first, second)
        return carry

    lax.fori_loop(0, rows // chunk, code_rows, 0)


def ask_kernel(owner, unit, asked):
    devices = asked.shape[0]
    units = owner.shape[1]
    blocks = 8
    rows = units * LG
    start = (unit[...] // blocks) * (LG * blocks) + unit[...] % blocks
    key = (lax.broadcasted_iota(jnp.int32, (1, units), 1) * rows + start).astype(jnp.float32)
    named = owner[...] == lax.broadcasted_iota(jnp.int32, (devices, units), 0)
    low = jnp.min(jnp.where(named, key, float(units * rows)), axis=1, keepdims=True)
    high = jnp.max(jnp.where(named, key, 0.0), axis=1, keepdims=True)
    low = low.astype(jnp.int32) & (rows - 1)
    high = high.astype(jnp.int32) & (rows - 1)
    asked[...] = jnp.broadcast_to(low | (high << 16), asked.shape)


def pack_kernel(asked, code, sent, row, starts, built, sem, sems):
    devices = built.shape[0]
    rows = code.shape[0] // PAIRS
    diagonal = lax.broadcasted_iota(jnp.int32, (BLOCK, BLOCK), 0) == lax.broadcasted_iota(
        jnp.int32, (BLOCK, BLOCK), 1
    )
    for i in range(devices // BLOCK):
        tile = jnp.where(diagonal, asked[pl.ds(i * BLOCK, BLOCK), :], 0)
        row[pl.ds(i, 1), :] = jnp.sum(tile, axis=0, keepdims=True)
    scalars = pltpu.make_async_copy(row, starts, sem)
    scalars.start()
    scalars.wait()
    part = devices // PACK_STEPS
    copies = []
    for step in range(PACK_STEPS):
        at = (step * part) % BLOCK

        def one(d, carry):
            both = starts[step * part // BLOCK, at + d]
            for j, start in enumerate((both & 0xFFFF, both >> 16)):
                for p in range(PAIRS):
                    built[step * part + d, pl.ds((j * PAIRS + p) * LG, LG), :] = code[
                        pl.ds(start + p * rows, LG, stride=8), :
                    ]
            return carry

        lax.fori_loop(0, part, one, 0, unroll=16)
        here = pl.ds(step * part, part)
        copies.append(pltpu.make_async_copy(built.at[here], sent.at[here], sems.at[step]))
        copies[-1].start()
    for copy in copies:
        copy.wait()


def prepare_kernel(h_frac, h_shift, v_frac, v_shift, weights, places, v_high, v_low):
    units = h_frac.shape[0]
    blocks, levels = v_frac.shape
    lane = lax.broadcasted_iota(jnp.int32, (units, BLOCK), 1)
    for k, weight in enumerate(cubic_weights(h_frac[...])):
        weights[pl.ds(k * units, units), :] = weight * DECODE
        places[pl.ds(k * units, units), :] = jnp.clip(lane + h_shift[...] + (k - 1), 0, BLOCK - 1)
    source = lax.broadcasted_iota(jnp.int32, (levels, levels), 0)
    target = lax.broadcasted_iota(jnp.int32, (1, levels), 1)

    def one_block(b, carry):
        vertical = jnp.zeros((levels, levels), jnp.float32)
        shift = v_shift[pl.ds(b, 1), :]
        for j, weight in enumerate(cubic_weights(v_frac[pl.ds(b, 1), :])):
            at = jnp.clip(target + shift + (j - 1), 0, levels - 1)
            vertical = vertical + jnp.where(source == at, weight * SPLIT, 0.0)
        high, low = halves(vertical.T)
        here = pl.ds(pl.multiple_of(b * levels, levels), levels)
        v_high[here, :] = high
        v_low[here, :] = low
        return carry

    lax.fori_loop(0, blocks, one_block, 0)


def lanes_at(value, index):
    numbers = lax.GatherDimensionNumbers(
        offset_dims=(),
        collapsed_slice_dims=(1,),
        start_index_map=(1,),
        operand_batching_dims=(0,),
        start_indices_batching_dims=(0,),
    )
    return lax.gather(
        value, index[..., None], numbers, (1, 1), mode=lax.GatherScatterMode.PROMISE_IN_BOUNDS
    )


def fifth_times(word, weight):
    y = word.astype(jnp.float32)
    square = y * y
    return (y * weight) * square * square


def advect_kernel(landing, got, weights, places, v_high, v_low, out, traced, moved_all, sems):
    units = places.shape[0] // 4
    levels = v_high.shape[1]
    blocks = v_high.shape[0] // levels
    groups = levels // LG
    rows = levels * blocks
    fields = 2 * PAIRS
    upper = lax.broadcasted_iota(jnp.int32, (2 * LG, BLOCK), 0) < LG

    def one_block(b, carry):
        base = b * (fields * levels)

        def two_units(step, inner):
            unit = [(step * 2 + i) * blocks + b for i in range(2)]
            row = [landing[u] * (PAIRS * LG) for u in unit]
            tails = [got[pl.ds(r + LG, 2 * LG), :] for r in row]
            words = [got[pl.ds(r, 2 * LG), :] for r in row]
            words.append(jnp.where(upper, pltpu.roll(tails[0], LG, 0), tails[1]))
            sums = [None] * 6
            for k in range(4):
                index = [places[pl.ds(u + k * units, 2 * LG, stride=0), :] for u in unit]
                weight = [weights[pl.ds(u + k * units, 2 * LG, stride=0), :] for u in unit]
                index.append(jnp.where(upper, index[0], index[1]))
                weight.append(jnp.where(upper, weight[0], weight[1]))
                for n in range(3):
                    word = lanes_at(words[n], index[n])
                    for half, part in enumerate((word, word << 16)):
                        term = fifth_times(part, weight[n])
                        at = n * 2 + half
                        sums[at] = term if k == 0 else sums[at] + term
            for n in range(2):
                for half in range(2):
                    for i in range(2):
                        f = i + half * PAIRS
                        traced[pl.ds(base + f * levels + (step * 2 + n) * LG, LG), :] = sums[n * 2 + half][
                            i * LG : (i + 1) * LG
                        ]
            for half in range(2):
                f = 2 + half * PAIRS
                at = pl.multiple_of(base + f * levels + step * 2 * LG, 2 * LG)
                traced[pl.ds(at, 2 * LG), :] = sums[4 + half]
            return inner

        lax.fori_loop(0, groups // 2, two_units, 0, unroll=UNROLL)
        return carry

    lax.fori_loop(0, blocks, one_block, 0)
    copies = []
    for first in range(0, fields, 2):

        def one_vertical(b, carry):
            at = pl.multiple_of(b * (fields * levels), levels)
            wide = jnp.concatenate(
                [traced[pl.ds(at + (first + i) * levels, levels), :] for i in range(2)], axis=1
            )
            t_high, t_low = halves(wide)
            here = pl.ds(pl.multiple_of(b * levels, levels), levels)
            high, low = v_high[here, :], v_low[here, :]
            moved = mxu(
                jnp.concatenate([high, high], axis=1), jnp.concatenate([t_high, t_low], axis=0), 1
            ) + mxu(low, t_high, 1)
            for i in range(2):
                moved_all[pl.ds((first + i) * rows + b, levels, stride=blocks), :] = moved[
                    :, i * BLOCK : (i + 1) * BLOCK
                ]
            return carry

        lax.fori_loop(0, blocks, one_vertical, 0, unroll=VERTICAL_UNROLL)
        here = pl.ds(first * rows, 2 * rows)
        copies.append(pltpu.make_async_copy(moved_all.at[here, :], out.at[here, :], sems.at[first // 2]))
        copies[-1].start()
    for copy in copies:
        copy.wait()


VMEM = pl.BlockSpec(memory_space=pltpu.VMEM)
SMEM = pl.BlockSpec(memory_space=pltpu.SMEM)
ANY = pl.BlockSpec(memory_space=pl.ANY)


def keep_near(value):
    return pltpu.with_memory_space_constraint(value, pltpu.VMEM)


def exchange(value):
    return lax.all_to_all(value, AXES, split_axis=0, concat_axis=0, tiled=True)


def heat(fields, sunlit, w_in, b_in, w_out, b_out, level_map):
    n_fields, levels, _, columns = fields.shape
    blocks = columns // BLOCK
    rows = levels * blocks
    return pl.pallas_call(
        heat_kernel,
        out_shape=(
            jax.ShapeDtypeStruct((rows, BLOCK), jnp.float32),
            jax.ShapeDtypeStruct((PAIRS * rows, BLOCK), jnp.int32),
        ),
        in_specs=[VMEM] * 7,
        out_specs=(VMEM, VMEM),
        compiler_params=pltpu.CompilerParams(vmem_limit_bytes=20 << 20),
        name="heat",
    )(
        *map(
            keep_far,
            (
                fields.reshape(n_fields * rows, BLOCK),
                sunlit.reshape(blocks, BLOCK),
                w_in,
                b_in.reshape(1, -1),
                w_out.T,
                b_out.reshape(1, -1),
                level_map.T,
            ),
        )
    )


def keep_far(value):
    return pltpu.with_memory_space_constraint(value, pltpu.HBM)


def ask(owner, unit, devices):
    return pl.pallas_call(
        ask_kernel,
        out_shape=jax.ShapeDtypeStruct((devices, BLOCK), jnp.int32),
        in_specs=[VMEM] * 2,
        out_specs=VMEM,
        name="ask",
    )(owner, unit)


def pack(asked, code):
    devices = asked.shape[0]
    shape = (devices, 2 * PAIRS * LG, BLOCK)
    return pl.pallas_call(
        pack_kernel,
        out_shape=jax.ShapeDtypeStruct(shape, jnp.int32),
        in_specs=[VMEM] * 2,
        out_specs=ANY,
        scratch_shapes=[
            pltpu.VMEM((devices // BLOCK, BLOCK), jnp.int32),
            pltpu.SMEM((devices // BLOCK, BLOCK), jnp.int32),
            pltpu.VMEM(shape, jnp.int32),
            pltpu.SemaphoreType.DMA,
            pltpu.SemaphoreType.DMA((PACK_STEPS,)),
        ],
        compiler_params=pltpu.CompilerParams(vmem_limit_bytes=12 << 20),
        name="pack",
    )(keep_near(asked), keep_near(code))


def prepare(h_frac, h_shift, v_frac, v_shift):
    units = h_frac.shape[0]
    blocks, levels = v_frac.shape
    return pl.pallas_call(
        prepare_kernel,
        out_shape=(
            jax.ShapeDtypeStruct((4 * units, BLOCK), jnp.float32),
            jax.ShapeDtypeStruct((4 * units, BLOCK), jnp.int32),
            jax.ShapeDtypeStruct((blocks * levels, levels), jnp.bfloat16),
            jax.ShapeDtypeStruct((blocks * levels, levels), jnp.bfloat16),
        ),
        in_specs=[VMEM] * 4,
        out_specs=(VMEM,) * 4,
        name="prepare",
    )(h_frac, h_shift, v_frac, v_shift)


def advect(landing, got, prepared):
    levels = prepared[2].shape[1]
    rows = prepared[2].shape[0]
    fields = 2 * PAIRS
    return pl.pallas_call(
        advect_kernel,
        out_shape=jax.ShapeDtypeStruct((fields * rows, BLOCK), jnp.float32),
        in_specs=[SMEM] + [VMEM] * 5,
        out_specs=ANY,
        scratch_shapes=[
            pltpu.VMEM((fields * rows, BLOCK), jnp.float32),
            pltpu.VMEM((fields * rows, BLOCK), jnp.float32),
            pltpu.SemaphoreType.DMA((PAIRS,)),
        ],
        name="advect",
    )(landing, keep_near(got.reshape(-1, BLOCK)), *prepared)


def per_device(
    fields,
    sunlit,
    w_in,
    b_in,
    w_out,
    b_out,
    level_map,
    dep_owner,
    owner_unit,
    h_frac,
    h_shift,
    v_frac,
    v_shift,
):
    n_fields, levels, _, columns = fields.shape
    units = owner_unit.shape[1]
    devices = lax.axis_size("lat") * lax.axis_size("lon")
    owners = dep_owner[0, :, 0]
    order = jnp.arange(units, dtype=jnp.int32)
    asked = exchange(ask(owners.reshape(1, units), owner_unit, devices)[:, None, :])
    second = jnp.any((owners[:, None] == owners[None, :]) & (order[:, None] > order[None, :]), axis=1)
    landing = owners * 2 + second.astype(jnp.int32)
    heating, code = heat(fields, sunlit, w_in, b_in, w_out, b_out, level_map)
    got = exchange(pack(asked.reshape(devices, BLOCK), code))
    prepared = prepare(h_frac[0], h_shift[0], v_frac[0], v_shift[0])
    advected = advect(landing, got, prepared)
    return (advected.reshape(n_fields, levels, 1, columns), heating.reshape(levels, 1, columns))


def solution(mesh):
    placed = (
        P(None, None, "lat", "lon"),
        P("lat", "lon"),
        P(),
        P(),
        P(),
        P(),
        P(),
        P("lat", "lon", None),
        P("lat", "lon"),
        P("lat", "lon", None),
        P("lat", "lon", None),
        P("lat", "lon", None),
        P("lat", "lon", None),
    )
    return jax.shard_map(
        per_device,
        mesh=mesh,
        in_specs=placed,
        out_specs=(P(None, None, "lat", "lon"), P(None, "lat", "lon")),
        check_vma=False,
    )
```

```python
import math

import jax
import jax.numpy as jnp
from jax import lax
from jax.experimental import pallas as pl
from jax.experimental.pallas import tpu as pltpu
from jax.sharding import PartitionSpec as P

BLOCK = 128
LG = 4
PAIRS = 3
TOGETHER = 4
VERTICAL_UNROLL = 8
PACK_STEPS = 4
AXES = ("lat", "lon")
CODE = 16480.0
SPLIT = 2.0**-75
DECODE = float((65536.0 * CODE) ** -5 / SPLIT)


def cubic_weights(fraction, scale=1.0):
    return (
        -fraction * (fraction - 1.0) * (fraction - 2.0) * (scale / 6.0),
        (fraction + 1.0) * (fraction - 1.0) * (fraction - 2.0) * (scale / 2.0),
        -(fraction + 1.0) * fraction * (fraction - 2.0) * (scale / 2.0),
        (fraction + 1.0) * fraction * (fraction - 1.0) * (scale / 6.0),
    )


def halves(value):
    high = value.astype(jnp.bfloat16)
    return high, (value - high.astype(jnp.float32)).astype(jnp.bfloat16)


def mxu(a, b, a_dim):
    return lax.dot_general(a, b, (((a_dim,), (0,)), ((), ())), preferred_element_type=jnp.float32)


def softplus(v):
    u = jnp.exp(-jnp.abs(v))
    return jnp.maximum(v, 0.0) + jnp.where(
        u < 0.005, u * (1.0 - u * (0.5 - u * (1.0 / 3.0))), jnp.log(1.0 + u)
    )


def coded(x):
    power = jnp.exp2(jnp.log(jnp.maximum(jnp.abs(x), 1e-30)) * (-0.8 / math.log(2.0)) + math.log2(65536.0 * CODE))
    return (x * power).astype(jnp.int32) + 32768


def word_of(first, second):
    low = lax.shift_right_logical(coded(second), 16)
    return ((coded(first) - low) & -65536) | low


def heat_kernel(x, sun, w_in, b_in, w_out, b_out, level_map, heat, code):
    outs, levels = level_map.shape
    hid, feats = w_in.shape
    blocks = sun.shape[0]
    width = 2 * BLOCK
    bias_in = jnp.broadcast_to(b_in[...], (width, hid)).T
    bias_out = jnp.broadcast_to(b_out[...], (width, outs)).T
    lower = (
        lax.broadcasted_iota(jnp.int32, (outs, outs), 0)
        >= lax.broadcasted_iota(jnp.int32, (outs, outs), 1)
    ).astype(jnp.float32).astype(jnp.bfloat16)
    map_high, map_low = halves(level_map[...])

    def two_blocks(step, carry):
        b = step * 2
        features = jnp.concatenate(
            [x[pl.ds(b + i, feats, stride=blocks), :] for i in range(2)], axis=1
        ).astype(jnp.bfloat16)
        hidden = jnp.tanh(mxu(w_in[...], features, 1) + bias_in).astype(jnp.bfloat16)
        optical = softplus(mxu(w_out[...], hidden, 0) + bias_out) * (4.0 / outs)
        high, rest = halves(optical)
        depth = mxu(lower, high, 1) + mxu(lower, rest, 1)
        high, rest = halves(optical * jnp.exp(-depth))
        warm = mxu(map_high, high, 0) + mxu(map_high, rest, 0) + mxu(map_low, high, 0)
        for i in range(2):
            lit = sun[pl.ds(b + i, 1), :].astype(jnp.float32)
            heat[pl.ds(b + i, levels, stride=blocks), :] = warm[:, i * BLOCK : (i + 1) * BLOCK] * lit
        return carry

    lax.fori_loop(0, blocks // 2, two_blocks, 0)
    rows = levels * blocks
    chunk = 64

    def code_rows(step, carry):
        at = pl.multiple_of(step * chunk, chunk)
        here = pl.ds(at, chunk)
        for p in range(PAIRS):
            first = x[pl.ds(at + p * rows, chunk), :]
            if p == 0:
                first = first + heat[here, :]
            second = x[pl.ds(at + (p + PAIRS) * rows, chunk), :]
            code[pl.ds(at + p * rows, chunk), :] = word_of(first, second)
        return carry

    lax.fori_loop(0, rows // chunk, code_rows, 0)


def ask_kernel(owner, unit, asked):
    devices = asked.shape[0]
    units = owner.shape[1]
    blocks = 8
    rows = units * LG
    start = (unit[...] // blocks) * (LG * blocks) + unit[...] % blocks
    key = (lax.broadcasted_iota(jnp.int32, (1, units), 1) * rows + start).astype(jnp.float32)
    named = owner[...] == lax.broadcasted_iota(jnp.int32, (devices, units), 0)
    low = jnp.min(jnp.where(named, key, float(units * rows)), axis=1, keepdims=True)
    high = jnp.max(jnp.where(named, key, 0.0), axis=1, keepdims=True)
    low = low.astype(jnp.int32) & (rows - 1)
    high = high.astype(jnp.int32) & (rows - 1)
    asked[...] = jnp.broadcast_to(low | (high << 16), asked.shape)


def pack_kernel(asked, code, sent, row, starts, built, sem, sems):
    devices = built.shape[0]
    rows = code.shape[0] // PAIRS
    diagonal = lax.broadcasted_iota(jnp.int32, (BLOCK, BLOCK), 0) == lax.broadcasted_iota(
        jnp.int32, (BLOCK, BLOCK), 1
    )
    for i in range(devices // BLOCK):
        tile = jnp.where(diagonal, asked[pl.ds(i * BLOCK, BLOCK), :], 0)
        row[pl.ds(i, 1), :] = jnp.sum(tile, axis=0, keepdims=True)
    scalars = pltpu.make_async_copy(row, starts, sem)
    scalars.start()
    scalars.wait()
    part = devices // PACK_STEPS
    copies = []
    for step in range(PACK_STEPS):
        at = (step * part) % BLOCK

        def one(d, carry):
            both = starts[step * part // BLOCK, at + d]
            for j, start in enumerate((both & 0xFFFF, both >> 16)):
                for p in range(PAIRS):
                    built[step * part + d, pl.ds((j * PAIRS + p) * LG, LG), :] = code[
                        pl.ds(start + p * rows, LG, stride=8), :
                    ]
            return carry

        lax.fori_loop(0, part, one, 0, unroll=16)
        here = pl.ds(step * part, part)
        copies.append(pltpu.make_async_copy(built.at[here], sent.at[here], sems.at[step]))
        copies[-1].start()
    for copy in copies:
        copy.wait()


def prepare_kernel(h_frac, h_shift, v_frac, v_shift, weights, places, v_high, v_low):
    units = h_frac.shape[0]
    blocks, levels = v_frac.shape
    lane = lax.broadcasted_iota(jnp.int32, (units, BLOCK), 1)
    for k, weight in enumerate(cubic_weights(h_frac[...])):
        weights[pl.ds(k * units, units), :] = weight * DECODE
        places[pl.ds(k * units, units), :] = jnp.clip(lane + h_shift[...] + (k - 1), 0, BLOCK - 1)
    source = lax.broadcasted_iota(jnp.int32, (levels, levels), 0)
    target = lax.broadcasted_iota(jnp.int32, (1, levels), 1)

    def one_block(b, carry):
        vertical = jnp.zeros((levels, levels), jnp.float32)
        shift = v_shift[pl.ds(b, 1), :]
        for j, weight in enumerate(cubic_weights(v_frac[pl.ds(b, 1), :])):
            at = jnp.clip(target + shift + (j - 1), 0, levels - 1)
            vertical = vertical + jnp.where(source == at, weight * SPLIT, 0.0)
        high, low = halves(vertical.T)
        here = pl.ds(pl.multiple_of(b * levels, levels), levels)
        v_high[here, :] = high
        v_low[here, :] = low
        return carry

    lax.fori_loop(0, blocks, one_block, 0)


def lanes_at(value, index):
    numbers = lax.GatherDimensionNumbers(
        offset_dims=(),
        collapsed_slice_dims=(1,),
        start_index_map=(1,),
        operand_batching_dims=(0,),
        start_indices_batching_dims=(0,),
    )
    return lax.gather(
        value, index[..., None], numbers, (1, 1), mode=lax.GatherScatterMode.PROMISE_IN_BOUNDS
    )


def fifth_times(word, weight):
    y = word.astype(jnp.float32)
    square = y * y
    return (y * weight) * square * square


def advect_kernel(landing, got, weights, places, v_high, v_low, out, traced, moved_all, sems):
    units = places.shape[0] // 4
    levels = v_high.shape[1]
    blocks = v_high.shape[0] // levels
    groups = levels // LG
    rows = levels * blocks
    fields = 2 * PAIRS
    upper = lax.broadcasted_iota(jnp.int32, (2 * LG, BLOCK), 0) < LG

    def some_blocks(turn, carry):
        def two_units(step, b, base):
            unit = [(step * 2 + i) * blocks + b for i in range(2)]
            row = [landing[u] * (PAIRS * LG) for u in unit]
            tails = [got[pl.ds(r + LG, 2 * LG), :] for r in row]
            words = [got[pl.ds(r, 2 * LG), :] for r in row]
            words.append(jnp.where(upper, pltpu.roll(tails[0], LG, 0), tails[1]))
            sums = [None] * 6
            for k in range(4):
                index = [places[pl.ds(u + k * units, 2 * LG, stride=0), :] for u in unit]
                weight = [weights[pl.ds(u + k * units, 2 * LG, stride=0), :] for u in unit]
                index.append(jnp.where(upper, index[0], index[1]))
                weight.append(jnp.where(upper, weight[0], weight[1]))
                for n in range(3):
                    word = lanes_at(words[n], index[n])
                    for half, part in enumerate((word, word << 16)):
                        term = fifth_times(part, weight[n])
                        at = n * 2 + half
                        sums[at] = term if k == 0 else sums[at] + term
            for n in range(2):
                for half in range(2):
                    for i in range(2):
                        f = i + half * PAIRS
                        traced[pl.ds(base + f * levels + (step * 2 + n) * LG, LG), :] = sums[n * 2 + half][
                            i * LG : (i + 1) * LG
                        ]
            for half in range(2):
                f = 2 + half * PAIRS
                at = pl.multiple_of(base + f * levels + step * 2 * LG, 2 * LG)
                traced[pl.ds(at, 2 * LG), :] = sums[4 + half]

        for i in range(TOGETHER):
            b = turn * TOGETHER + i
            for step in range(groups // 2):
                two_units(step, b, b * (fields * levels))
        return carry

    lax.fori_loop(0, blocks // TOGETHER, some_blocks, 0)
    copies = []
    for first in range(0, fields, 2):

        def one_vertical(b, carry):
            at = pl.multiple_of(b * (fields * levels), levels)
            wide = jnp.concatenate(
                [traced[pl.ds(at + (first + i) * levels, levels), :] for i in range(2)], axis=1
            )
            t_high, t_low = halves(wide)
            here = pl.ds(pl.multiple_of(b * levels, levels), levels)
            high, low = v_high[here, :], v_low[here, :]
            moved = mxu(
                jnp.concatenate([high, high], axis=1), jnp.concatenate([t_high, t_low], axis=0), 1
            ) + mxu(low, t_high, 1)
            for i in range(2):
                moved_all[pl.ds((first + i) * rows + b, levels, stride=blocks), :] = moved[
                    :, i * BLOCK : (i + 1) * BLOCK
                ]
            return carry

        lax.fori_loop(0, blocks, one_vertical, 0, unroll=VERTICAL_UNROLL)
        here = pl.ds(first * rows, 2 * rows)
        copies.append(pltpu.make_async_copy(moved_all.at[here, :], out.at[here, :], sems.at[first // 2]))
        copies[-1].start()
    for copy in copies:
        copy.wait()


VMEM = pl.BlockSpec(memory_space=pltpu.VMEM)
SMEM = pl.BlockSpec(memory_space=pltpu.SMEM)
ANY = pl.BlockSpec(memory_space=pl.ANY)


def keep_near(value):
    return pltpu.with_memory_space_constraint(value, pltpu.VMEM)


def exchange(value):
    return lax.all_to_all(value, AXES, split_axis=0, concat_axis=0, tiled=True)


def heat(fields, sunlit, w_in, b_in, w_out, b_out, level_map):
    n_fields, levels, _, columns = fields.shape
    blocks = columns // BLOCK
    rows = levels * blocks
    return pl.pallas_call(
        heat_kernel,
        out_shape=(
            jax.ShapeDtypeStruct((rows, BLOCK), jnp.float32),
            jax.ShapeDtypeStruct((PAIRS * rows, BLOCK), jnp.int32),
        ),
        in_specs=[VMEM] * 7,
        out_specs=(VMEM, VMEM),
        compiler_params=pltpu.CompilerParams(vmem_limit_bytes=20 << 20),
        name="heat",
    )(
        *map(
            keep_far,
            (
                fields.reshape(n_fields * rows, BLOCK),
                sunlit.reshape(blocks, BLOCK),
                w_in,
                b_in.reshape(1, -1),
                w_out.T,
                b_out.reshape(1, -1),
                level_map.T,
            ),
        )
    )


def keep_far(value):
    return pltpu.with_memory_space_constraint(value, pltpu.HBM)


def ask(owner, unit, devices):
    return pl.pallas_call(
        ask_kernel,
        out_shape=jax.ShapeDtypeStruct((devices, BLOCK), jnp.int32),
        in_specs=[VMEM] * 2,
        out_specs=VMEM,
        name="ask",
    )(owner, unit)


def pack(asked, code):
    devices = asked.shape[0]
    shape = (devices, 2 * PAIRS * LG, BLOCK)
    return pl.pallas_call(
        pack_kernel,
        out_shape=jax.ShapeDtypeStruct(shape, jnp.int32),
        in_specs=[VMEM] * 2,
        out_specs=ANY,
        scratch_shapes=[
            pltpu.VMEM((devices // BLOCK, BLOCK), jnp.int32),
            pltpu.SMEM((devices // BLOCK, BLOCK), jnp.int32),
            pltpu.VMEM(shape, jnp.int32),
            pltpu.SemaphoreType.DMA,
            pltpu.SemaphoreType.DMA((PACK_STEPS,)),
        ],
        compiler_params=pltpu.CompilerParams(vmem_limit_bytes=12 << 20),
        name="pack",
    )(keep_near(asked), keep_near(code))


def prepare(h_frac, h_shift, v_frac, v_shift):
    units = h_frac.shape[0]
    blocks, levels = v_frac.shape
    return pl.pallas_call(
        prepare_kernel,
        out_shape=(
            jax.ShapeDtypeStruct((4 * units, BLOCK), jnp.float32),
            jax.ShapeDtypeStruct((4 * units, BLOCK), jnp.int32),
            jax.ShapeDtypeStruct((blocks * levels, levels), jnp.bfloat16),
            jax.ShapeDtypeStruct((blocks * levels, levels), jnp.bfloat16),
        ),
        in_specs=[VMEM] * 4,
        out_specs=(VMEM,) * 4,
        name="prepare",
    )(h_frac, h_shift, v_frac, v_shift)


def advect(landing, got, prepared):
    levels = prepared[2].shape[1]
    rows = prepared[2].shape[0]
    fields = 2 * PAIRS
    return pl.pallas_call(
        advect_kernel,
        out_shape=jax.ShapeDtypeStruct((fields * rows, BLOCK), jnp.float32),
        in_specs=[SMEM] + [VMEM] * 5,
        out_specs=ANY,
        scratch_shapes=[
            pltpu.VMEM((fields * rows, BLOCK), jnp.float32),
            pltpu.VMEM((fields * rows, BLOCK), jnp.float32),
            pltpu.SemaphoreType.DMA((PAIRS,)),
        ],
        name="advect",
    )(landing, keep_near(got.reshape(-1, BLOCK)), *prepared)


def per_device(
    fields,
    sunlit,
    w_in,
    b_in,
    w_out,
    b_out,
    level_map,
    dep_owner,
    owner_unit,
    h_frac,
    h_shift,
    v_frac,
    v_shift,
):
    n_fields, levels, _, columns = fields.shape
    units = owner_unit.shape[1]
    devices = lax.axis_size("lat") * lax.axis_size("lon")
    owners = dep_owner[0, :, 0]
    order = jnp.arange(units, dtype=jnp.int32)
    asked = exchange(ask(owners.reshape(1, units), owner_unit, devices)[:, None, :])
    second = jnp.any((owners[:, None] == owners[None, :]) & (order[:, None] > order[None, :]), axis=1)
    landing = owners * 2 + second.astype(jnp.int32)
    heating, code = heat(fields, sunlit, w_in, b_in, w_out, b_out, level_map)
    got = exchange(pack(asked.reshape(devices, BLOCK), code))
    prepared = prepare(h_frac[0], h_shift[0], v_frac[0], v_shift[0])
    advected = advect(landing, got, prepared)
    return (advected.reshape(n_fields, levels, 1, columns), heating.reshape(levels, 1, columns))


def solution(mesh):
    placed = (
        P(None, None, "lat", "lon"),
        P("lat", "lon"),
        P(),
        P(),
        P(),
        P(),
        P(),
        P("lat", "lon", None),
        P("lat", "lon"),
        P("lat", "lon", None),
        P("lat", "lon", None),
        P("lat", "lon", None),
        P("lat", "lon", None),
    )
    return jax.shard_map(
        per_device,
        mesh=mesh,
        in_specs=placed,
        out_specs=(P(None, None, "lat", "lon"), P(None, "lat", "lon")),
        check_vma=False,
    )
```

```python
import math

import jax
import jax.numpy as jnp
from jax import lax
from jax.experimental import pallas as pl
from jax.experimental.pallas import tpu as pltpu
from jax.sharding import PartitionSpec as P

BLOCK = 128
LG = 4
PAIRS = 3
TOGETHER = 8
VERTICAL_UNROLL = 8
PACK_STEPS = 4
AXES = ("lat", "lon")
CODE = 16480.0
SPLIT = 2.0**-75
DECODE = float((65536.0 * CODE) ** -5 / SPLIT)


def cubic_weights(fraction, scale=1.0):
    return (
        -fraction * (fraction - 1.0) * (fraction - 2.0) * (scale / 6.0),
        (fraction + 1.0) * (fraction - 1.0) * (fraction - 2.0) * (scale / 2.0),
        -(fraction + 1.0) * fraction * (fraction - 2.0) * (scale / 2.0),
        (fraction + 1.0) * fraction * (fraction - 1.0) * (scale / 6.0),
    )


def halves(value):
    high = value.astype(jnp.bfloat16)
    return high, (value - high.astype(jnp.float32)).astype(jnp.bfloat16)


def mxu(a, b, a_dim):
    return lax.dot_general(a, b, (((a_dim,), (0,)), ((), ())), preferred_element_type=jnp.float32)


def softplus(v):
    u = jnp.exp(-jnp.abs(v))
    return jnp.maximum(v, 0.0) + jnp.where(
        u < 0.005, u * (1.0 - u * (0.5 - u * (1.0 / 3.0))), jnp.log(1.0 + u)
    )


def coded(x):
    power = jnp.exp2(jnp.log(jnp.maximum(jnp.abs(x), 1e-30)) * (-0.8 / math.log(2.0)) + math.log2(65536.0 * CODE))
    return (x * power).astype(jnp.int32) + 32768


def word_of(first, second):
    low = lax.shift_right_logical(coded(second), 16)
    return ((coded(first) - low) & -65536) | low


def heat_kernel(x, sun, w_in, b_in, w_out, b_out, level_map, heat, code):
    outs, levels = level_map.shape
    hid, feats = w_in.shape
    blocks = sun.shape[0]
    width = 2 * BLOCK
    bias_in = jnp.broadcast_to(b_in[...], (width, hid)).T
    bias_out = jnp.broadcast_to(b_out[...], (width, outs)).T
    lower = (
        lax.broadcasted_iota(jnp.int32, (outs, outs), 0)
        >= lax.broadcasted_iota(jnp.int32, (outs, outs), 1)
    ).astype(jnp.float32).astype(jnp.bfloat16)
    map_high, map_low = halves(level_map[...])

    def two_blocks(step, carry):
        b = step * 2
        features = jnp.concatenate(
            [x[pl.ds(b + i, feats, stride=blocks), :] for i in range(2)], axis=1
        ).astype(jnp.bfloat16)
        hidden = jnp.tanh(mxu(w_in[...], features, 1) + bias_in).astype(jnp.bfloat16)
        optical = softplus(mxu(w_out[...], hidden, 0) + bias_out) * (4.0 / outs)
        high, rest = halves(optical)
        depth = mxu(lower, high, 1) + mxu(lower, rest, 1)
        high, rest = halves(optical * jnp.exp(-depth))
        warm = mxu(map_high, high, 0) + mxu(map_high, rest, 0) + mxu(map_low, high, 0)
        for i in range(2):
            lit = sun[pl.ds(b + i, 1), :].astype(jnp.float32)
            heat[pl.ds(b + i, levels, stride=blocks), :] = warm[:, i * BLOCK : (i + 1) * BLOCK] * lit
        return carry

    lax.fori_loop(0, blocks // 2, two_blocks, 0)
    rows = levels * blocks
    chunk = 64

    def code_rows(step, carry):
        at = pl.multiple_of(step * chunk, chunk)
        here = pl.ds(at, chunk)
        for p in range(PAIRS):
            first = x[pl.ds(at + p * rows, chunk), :]
            if p == 0:
                first = first + heat[here, :]
            second = x[pl.ds(at + (p + PAIRS) * rows, chunk), :]
            code[pl.ds(at + p * rows, chunk), :] = word_of(first, second)
        return carry

    lax.fori_loop(0, rows // chunk, code_rows, 0)


def ask_kernel(owner, unit, asked):
    devices = asked.shape[0]
    units = owner.shape[1]
    blocks = 8
    rows = units * LG
    start = (unit[...] // blocks) * (LG * blocks) + unit[...] % blocks
    key = (lax.broadcasted_iota(jnp.int32, (1, units), 1) * rows + start).astype(jnp.float32)
    named = owner[...] == lax.broadcasted_iota(jnp.int32, (devices, units), 0)
    low = jnp.min(jnp.where(named, key, float(units * rows)), axis=1, keepdims=True)
    high = jnp.max(jnp.where(named, key, 0.0), axis=1, keepdims=True)
    low = low.astype(jnp.int32) & (rows - 1)
    high = high.astype(jnp.int32) & (rows - 1)
    asked[...] = jnp.broadcast_to(low | (high << 16), asked.shape)


def pack_kernel(asked, code, sent, row, starts, built, sem, sems):
    devices = built.shape[0]
    rows = code.shape[0] // PAIRS
    diagonal = lax.broadcasted_iota(jnp.int32, (BLOCK, BLOCK), 0) == lax.broadcasted_iota(
        jnp.int32, (BLOCK, BLOCK), 1
    )
    for i in range(devices // BLOCK):
        tile = jnp.where(diagonal, asked[pl.ds(i * BLOCK, BLOCK), :], 0)
        row[pl.ds(i, 1), :] = jnp.sum(tile, axis=0, keepdims=True)
    scalars = pltpu.make_async_copy(row, starts, sem)
    scalars.start()
    scalars.wait()
    part = devices // PACK_STEPS
    copies = []
    for step in range(PACK_STEPS):
        at = (step * part) % BLOCK

        def one(d, carry):
            both = starts[step * part // BLOCK, at + d]
            for j, start in enumerate((both & 0xFFFF, both >> 16)):
                for p in range(PAIRS):
                    built[step * part + d, pl.ds((j * PAIRS + p) * LG, LG), :] = code[
                        pl.ds(start + p * rows, LG, stride=8), :
                    ]
            return carry

        lax.fori_loop(0, part, one, 0, unroll=32)
        here = pl.ds(step * part, part)
        copies.append(pltpu.make_async_copy(built.at[here], sent.at[here], sems.at[step]))
        copies[-1].start()
    for copy in copies:
        copy.wait()


def prepare_kernel(h_frac, h_shift, v_frac, v_shift, weights, places, v_high, v_low):
    units = h_frac.shape[0]
    blocks, levels = v_frac.shape
    lane = lax.broadcasted_iota(jnp.int32, (units, BLOCK), 1)
    for k, weight in enumerate(cubic_weights(h_frac[...])):
        weights[pl.ds(k * units, units), :] = weight * DECODE
        places[pl.ds(k * units, units), :] = jnp.clip(lane + h_shift[...] + (k - 1), 0, BLOCK - 1)
    source = lax.broadcasted_iota(jnp.int32, (levels, levels), 0)
    target = lax.broadcasted_iota(jnp.int32, (1, levels), 1)

    def one_block(b, carry):
        vertical = jnp.zeros((levels, levels), jnp.float32)
        shift = v_shift[pl.ds(b, 1), :]
        for j, weight in enumerate(cubic_weights(v_frac[pl.ds(b, 1), :])):
            at = jnp.clip(target + shift + (j - 1), 0, levels - 1)
            vertical = vertical + jnp.where(source == at, weight * SPLIT, 0.0)
        high, low = halves(vertical.T)
        here = pl.ds(pl.multiple_of(b * levels, levels), levels)
        v_high[here, :] = high
        v_low[here, :] = low
        return carry

    lax.fori_loop(0, blocks, one_block, 0)


def lanes_at(value, index):
    numbers = lax.GatherDimensionNumbers(
        offset_dims=(),
        collapsed_slice_dims=(1,),
        start_index_map=(1,),
        operand_batching_dims=(0,),
        start_indices_batching_dims=(0,),
    )
    return lax.gather(
        value, index[..., None], numbers, (1, 1), mode=lax.GatherScatterMode.PROMISE_IN_BOUNDS
    )


def fifth_times(word, weight):
    y = word.astype(jnp.float32)
    square = y * y
    return (y * weight) * square * square


def advect_kernel(landing, got, weights, places, v_high, v_low, out, traced, moved_all, sems):
    units = places.shape[0] // 4
    levels = v_high.shape[1]
    blocks = v_high.shape[0] // levels
    groups = levels // LG
    rows = levels * blocks
    fields = 2 * PAIRS
    upper = lax.broadcasted_iota(jnp.int32, (2 * LG, BLOCK), 0) < LG

    def some_blocks(turn, carry):
        def two_units(step, b, base):
            unit = [(step * 2 + i) * blocks + b for i in range(2)]
            row = [landing[u] * (PAIRS * LG) for u in unit]
            tails = [got[pl.ds(r + LG, 2 * LG), :] for r in row]
            words = [got[pl.ds(r, 2 * LG), :] for r in row]
            words.append(jnp.where(upper, pltpu.roll(tails[0], LG, 0), tails[1]))
            sums = [None] * 6
            for k in range(4):
                index = [places[pl.ds(u + k * units, 2 * LG, stride=0), :] for u in unit]
                weight = [weights[pl.ds(u + k * units, 2 * LG, stride=0), :] for u in unit]
                index.append(jnp.where(upper, index[0], index[1]))
                weight.append(jnp.where(upper, weight[0], weight[1]))
                for n in range(3):
                    word = lanes_at(words[n], index[n])
                    for half, part in enumerate((word, word << 16)):
                        term = fifth_times(part, weight[n])
                        at = n * 2 + half
                        sums[at] = term if k == 0 else sums[at] + term
            for n in range(2):
                for half in range(2):
                    for i in range(2):
                        f = i + half * PAIRS
                        traced[pl.ds(base + f * levels + (step * 2 + n) * LG, LG), :] = sums[n * 2 + half][
                            i * LG : (i + 1) * LG
                        ]
            for half in range(2):
                f = 2 + half * PAIRS
                at = pl.multiple_of(base + f * levels + step * 2 * LG, 2 * LG)
                traced[pl.ds(at, 2 * LG), :] = sums[4 + half]

        for i in range(TOGETHER):
            b = turn * TOGETHER + i
            for step in range(groups // 2):
                two_units(step, b, b * (fields * levels))
        return carry

    lax.fori_loop(0, blocks // TOGETHER, some_blocks, 0)
    copies = []
    for first in range(0, fields, 2):

        def one_vertical(b, carry):
            at = pl.multiple_of(b * (fields * levels), levels)
            wide = jnp.concatenate(
                [traced[pl.ds(at + (first + i) * levels, levels), :] for i in range(2)], axis=1
            )
            t_high, t_low = halves(wide)
            here = pl.ds(pl.multiple_of(b * levels, levels), levels)
            high, low = v_high[here, :], v_low[here, :]
            moved = mxu(
                jnp.concatenate([high, high], axis=1), jnp.concatenate([t_high, t_low], axis=0), 1
            ) + mxu(low, t_high, 1)
            for i in range(2):
                moved_all[pl.ds((first + i) * rows + b, levels, stride=blocks), :] = moved[
                    :, i * BLOCK : (i + 1) * BLOCK
                ]
            return carry

        lax.fori_loop(0, blocks, one_vertical, 0, unroll=VERTICAL_UNROLL)
        here = pl.ds(first * rows, 2 * rows)
        copies.append(pltpu.make_async_copy(moved_all.at[here, :], out.at[here, :], sems.at[first // 2]))
        copies[-1].start()
    for copy in copies:
        copy.wait()


VMEM = pl.BlockSpec(memory_space=pltpu.VMEM)
SMEM = pl.BlockSpec(memory_space=pltpu.SMEM)
ANY = pl.BlockSpec(memory_space=pl.ANY)


def keep_near(value):
    return pltpu.with_memory_space_constraint(value, pltpu.VMEM)


def exchange(value):
    return lax.all_to_all(value, AXES, split_axis=0, concat_axis=0, tiled=True)


def heat(fields, sunlit, w_in, b_in, w_out, b_out, level_map):
    n_fields, levels, _, columns = fields.shape
    blocks = columns // BLOCK
    rows = levels * blocks
    return pl.pallas_call(
        heat_kernel,
        out_shape=(
            jax.ShapeDtypeStruct((rows, BLOCK), jnp.float32),
            jax.ShapeDtypeStruct((PAIRS * rows, BLOCK), jnp.int32),
        ),
        in_specs=[VMEM] * 7,
        out_specs=(VMEM, VMEM),
        compiler_params=pltpu.CompilerParams(vmem_limit_bytes=20 << 20),
        name="heat",
    )(
        *map(
            keep_far,
            (
                fields.reshape(n_fields * rows, BLOCK),
                sunlit.reshape(blocks, BLOCK),
                w_in,
                b_in.reshape(1, -1),
                w_out.T,
                b_out.reshape(1, -1),
                level_map.T,
            ),
        )
    )


def keep_far(value):
    return pltpu.with_memory_space_constraint(value, pltpu.HBM)


def ask(owner, unit, devices):
    return pl.pallas_call(
        ask_kernel,
        out_shape=jax.ShapeDtypeStruct((devices, BLOCK), jnp.int32),
        in_specs=[VMEM] * 2,
        out_specs=VMEM,
        name="ask",
    )(owner, unit)


def pack(asked, code):
    devices = asked.shape[0]
    shape = (devices, 2 * PAIRS * LG, BLOCK)
    return pl.pallas_call(
        pack_kernel,
        out_shape=jax.ShapeDtypeStruct(shape, jnp.int32),
        in_specs=[VMEM] * 2,
        out_specs=ANY,
        scratch_shapes=[
            pltpu.VMEM((devices // BLOCK, BLOCK), jnp.int32),
            pltpu.SMEM((devices // BLOCK, BLOCK), jnp.int32),
            pltpu.VMEM(shape, jnp.int32),
            pltpu.SemaphoreType.DMA,
            pltpu.SemaphoreType.DMA((PACK_STEPS,)),
        ],
        compiler_params=pltpu.CompilerParams(vmem_limit_bytes=12 << 20),
        name="pack",
    )(keep_near(asked), keep_near(code))


def prepare(h_frac, h_shift, v_frac, v_shift):
    units = h_frac.shape[0]
    blocks, levels = v_frac.shape
    return pl.pallas_call(
        prepare_kernel,
        out_shape=(
            jax.ShapeDtypeStruct((4 * units, BLOCK), jnp.float32),
            jax.ShapeDtypeStruct((4 * units, BLOCK), jnp.int32),
            jax.ShapeDtypeStruct((blocks * levels, levels), jnp.bfloat16),
            jax.ShapeDtypeStruct((blocks * levels, levels), jnp.bfloat16),
        ),
        in_specs=[VMEM] * 4,
        out_specs=(VMEM,) * 4,
        name="prepare",
    )(h_frac, h_shift, v_frac, v_shift)


def advect(landing, got, prepared):
    levels = prepared[2].shape[1]
    rows = prepared[2].shape[0]
    fields = 2 * PAIRS
    return pl.pallas_call(
        advect_kernel,
        out_shape=jax.ShapeDtypeStruct((fields * rows, BLOCK), jnp.float32),
        in_specs=[SMEM] + [VMEM] * 5,
        out_specs=ANY,
        scratch_shapes=[
            pltpu.VMEM((fields * rows, BLOCK), jnp.float32),
            pltpu.VMEM((fields * rows, BLOCK), jnp.float32),
            pltpu.SemaphoreType.DMA((PAIRS,)),
        ],
        name="advect",
    )(landing, keep_near(got.reshape(-1, BLOCK)), *prepared)


def per_device(
    fields,
    sunlit,
    w_in,
    b_in,
    w_out,
    b_out,
    level_map,
    dep_owner,
    owner_unit,
    h_frac,
    h_shift,
    v_frac,
    v_shift,
):
    n_fields, levels, _, columns = fields.shape
    units = owner_unit.shape[1]
    devices = lax.axis_size("lat") * lax.axis_size("lon")
    owners = dep_owner[0, :, 0]
    order = jnp.arange(units, dtype=jnp.int32)
    asked = exchange(ask(owners.reshape(1, units), owner_unit, devices)[:, None, :])
    second = jnp.any((owners[:, None] == owners[None, :]) & (order[:, None] > order[None, :]), axis=1)
    landing = owners * 2 + second.astype(jnp.int32)
    heating, code = heat(fields, sunlit, w_in, b_in, w_out, b_out, level_map)
    got = exchange(pack(asked.reshape(devices, BLOCK), code))
    prepared = prepare(h_frac[0], h_shift[0], v_frac[0], v_shift[0])
    advected = advect(landing, got, prepared)
    return (advected.reshape(n_fields, levels, 1, columns), heating.reshape(levels, 1, columns))


def solution(mesh):
    placed = (
        P(None, None, "lat", "lon"),
        P("lat", "lon"),
        P(),
        P(),
        P(),
        P(),
        P(),
        P("lat", "lon", None),
        P("lat", "lon"),
        P("lat", "lon", None),
        P("lat", "lon", None),
        P("lat", "lon", None),
        P("lat", "lon", None),
    )
    return jax.shard_map(
        per_device,
        mesh=mesh,
        in_specs=placed,
        out_specs=(P(None, None, "lat", "lon"), P(None, "lat", "lon")),
        check_vma=False,
    )
```
